32 devices in a mesh: gx: 8 (over y, x, core), gy: 4 (over z).
Axes of the slice: x: 2, y: 2, z: 4, core: 2. Of those that a mesh axis runs over, the one named last changes fastest.
Arguments:
- history: bfloat16 [4, 2048, 2048], P(None, 'gx', 'gy'), may hold values from -6 to 6
- start_x: float32 [2048, 256], P('gx'), may hold values from -6 to 6
- start_y: float32 [2048, 256], P('gy'), may hold values from -6 to 6
Outputs:
- core: float32 [4, 256, 256], P(None, 'gx', 'gy')
The draws below stay inside these ranges and needn't reach their ends.
All inputs are finite; a program needn't handle non-finite values.
Results may differ from the reference program's by a relative error of at most 0.0027.
Values may be sent and summed in bfloat16 or wider, within the bound.
A program may use at most 128 MiB of HBM per device.

```python
import jax
import jax.numpy as jnp
from jax import lax

NX = 2048
NY = 2048
RANK = 256
SLABS = 4
ITERS = 3


def level_of(stream_key, extent, pieces, least, high):
    def one(dim, parts):
        steps = jax.random.uniform(jax.random.fold_in(jax.random.fold_in(stream_key, 6), dim), (parts,), jnp.float32, least / len(pieces), high / len(pieces))
        return jnp.repeat(jnp.exp(steps), extent[dim] // parts).reshape((-1,) + (1,) * (len(extent) - dim - 1))

    gain = one(*pieces[0])
    for cut in pieces[1:]:
        gain = gain * one(*cut)
    return gain


def noise(key, extent, scale, limit, split=(), kind=jnp.bfloat16):
    drawn = scale * jax.random.normal(key, extent, jnp.float32)
    if split:
        drawn = drawn * level_of(key, extent, split, -0.22, 0.18)
    return jnp.clip(drawn, -limit, limit).astype(kind)


def setup_inputs(seed: int = 0) -> dict:
    key_list = jax.random.split(jax.random.key(seed), 4)
    return {
        "history": noise(key_list[0], (SLABS, NX, NY), 1.0, 6.0, ((1, 8), (2, 4))),
        "start_x": noise(key_list[1], (NX, RANK), 1.0, 6.0, ((0, 8),), jnp.float32),
        "start_y": noise(key_list[2], (NY, RANK), 1.0, 6.0, ((0, 4),), jnp.float32),
    }


def subspace(gram, start):
    basis = start
    for step in range(ITERS):
        image = jnp.dot(gram.astype(jnp.float32), basis.astype(jnp.float32), precision=lax.Precision.HIGHEST, preferred_element_type=jnp.float32)
        inner = jnp.dot(image.T.astype(jnp.float32), image.astype(jnp.float32), precision=lax.Precision.HIGHEST, preferred_element_type=jnp.float32)
        lower = jnp.linalg.cholesky(inner)
        basis = lax.linalg.triangular_solve(lower, image, left_side=False, lower=True, transpose_a=True)
    return basis

def reference(history, start_x, start_y):
    data = history.astype(jnp.float32)
    by_x = jnp.transpose(data, (1, 0, 2)).reshape(NX, SLABS * NY)
    gram_x = jnp.dot(by_x.astype(jnp.float32), by_x.T.astype(jnp.float32), precision=lax.Precision.HIGHEST, preferred_element_type=jnp.float32)
    by_y = jnp.transpose(data, (2, 0, 1)).reshape(NY, SLABS * NX)
    gram_y = jnp.dot(by_y.astype(jnp.float32), by_y.T.astype(jnp.float32), precision=lax.Precision.HIGHEST, preferred_element_type=jnp.float32)
    basis_x = subspace(gram_x, start_x)
    basis_y = subspace(gram_y, start_y)
    factor_x = lax.optimization_barrier(basis_x.astype(jnp.bfloat16)).astype(jnp.float32)
    factor_y = lax.optimization_barrier(basis_y.astype(jnp.bfloat16)).astype(jnp.float32)
    partial_core = jnp.einsum('sxy,yb->sxb', data, factor_y, precision=lax.Precision.HIGHEST)
    core = jnp.einsum('xa,sxb->sab', factor_x, partial_core, precision=lax.Precision.HIGHEST)
    return core
```

```python
import functools

import jax
import jax.numpy as jnp
from jax import lax
from jax.experimental import pallas as pl
from jax.experimental.pallas import tpu as pltpu
from jax.sharding import PartitionSpec as P

ITERS = 3
BLOCK = 64
HIGHEST = lax.Precision.HIGHEST
MESH = pl.DeviceIdType.MESH
F32, BF16 = jnp.float32, jnp.bfloat16
NN, NT, TN = ((1,), (0,)), ((1,), (1,)), ((0,), (0,))


def mul(a, b, dims):
    return lax.dot_general(a, b, (dims, ((), ())), precision=HIGHEST, preferred_element_type=F32)


def bdot(a, b, dims):
    return lax.dot_general(a, b, (dims, ((), ())), preferred_element_type=F32)


def split(v):
    hi = v.astype(BF16)
    return hi, (v - hi.astype(F32)).astype(BF16)


def dot3(a, b, dims):
    return bdot(a[0], b[0], dims) + (bdot(a[0], b[1], dims) + bdot(a[1], b[0], dims))


def eliminate(block):
    size = block.shape[0]
    sub = lax.broadcasted_iota(jnp.int32, (size, size), 0)
    lane = lax.broadcasted_iota(jnp.int32, (size, size), 1)
    eye = jnp.where(sub == lane, 1.0, 0.0).astype(F32)
    sub8 = lax.broadcasted_iota(jnp.int32, (8, 1), 0)
    whole = jnp.concatenate([block, eye], axis=1)
    rows = [whole[t * 8 : t * 8 + 8] for t in range(size // 8)]
    for k in range(0, size, 2):
        home, at = k // 8, k % 8
        held = rows[home]
        row0, row1 = held[at : at + 1, :], held[at + 1 : at + 2, :]
        inv0 = 1.0 / row0[:, k : k + 1]
        cross = row0[:, k + 1 : k + 2]
        ratio = cross * inv0
        inv1 = 1.0 / (row1[:, k + 1 : k + 2] - ratio * cross)
        scaled0 = row0 * inv0
        scaled1 = (row1 - ratio * row0) * inv1
        for t in range(home, size // 8):
            col0 = rows[t][:, k : k + 1]
            col1 = rows[t][:, k + 1 : k + 2] - ratio * col0
            if t == home:
                col0 = jnp.where(sub8 > at, col0, 0.0)
                col1 = jnp.where(sub8 > at + 1, col1, 0.0)
            rows[t] = rows[t] - col0 * scaled0 - col1 * scaled1
    whole = jnp.concatenate(rows, axis=0)
    diag = jnp.sum(jnp.where(sub == lane, whole[:, :size], 0.0), axis=1, keepdims=True)
    return whole[:, size:] * (1.0 / jnp.sqrt(diag))


def inverse_factor(inner, work, out_ref):
    rank = inner.shape[0]
    sub = lax.broadcasted_iota(jnp.int32, (rank, rank), 0)
    lane = lax.broadcasted_iota(jnp.int32, (rank, rank), 1)
    same = sub == lane
    diag = jnp.where(same, inner, 0.0)
    tall = 1.0 / jnp.sqrt(jnp.sum(diag, axis=1, keepdims=True))
    wide = 1.0 / jnp.sqrt(jnp.sum(diag, axis=0, keepdims=True))
    work[:, :rank] = inner * tall * wide
    work[:, rank:] = jnp.where(same, 1.0, 0.0).astype(F32)
    for at in range(0, rank, BLOCK):
        inverse = eliminate(work[at : at + BLOCK, at : at + BLOCK])
        top = mul(inverse, work[at : at + BLOCK, :], NN)
        out_ref[at : at + BLOCK, :] = top[:, rank:] * wide
        if at + BLOCK < rank:
            left = top[:, at + BLOCK : rank]
            work[at + BLOCK :, :] = work[at + BLOCK :, :] - mul(left, top, TN)


def kernel(
    n, h_ref, bx_ref, by_ref, out_ref,
    hw, ghi, glo, begin, bhi, blo, part, rslots, image, ipart, islots, inner, work, linv, fxt, fy, wsum, cpart, oslots,
    own, bs, br, bzs, bzr, bps, bpr, xs, xr, zr, zl, ks, yr, rs, rr, as_, ar, ps, pr, i1s, i1r, i2s, i2r, fs, fr, os_, or_,
):
    i, j = lax.axis_index("gx"), lax.axis_index("gy")
    p, c = i // 2, lax.rem(i, 2)
    even = c == 0
    odd = c == 1
    slabs, hrows, hcols = h_ref.shape
    rank = bx_ref.shape[1]
    chunk = image.shape[3]
    irows = rank // n
    sibling = (i + 1 - 2 * c, j)

    def mod(v):
        return lax.rem(v + n, n)

    def rc(src, dst, ss, rsem, dev):
        return pltpu.make_async_remote_copy(
            src_ref=src, dst_ref=dst, send_sem=ss, recv_sem=rsem, device_id=dev, device_id_type=MESH
        )

    a = jnp.where(even, p, j)
    r = jnp.where(even, j, p)

    def dev(aa, rr_):
        return (jnp.where(even, 2 * aa, 2 * rr_ + 1), jnp.where(even, rr_, aa))

    def place(pp, jj):
        return jnp.where(even, pp, jj), jnp.where(even, jj, pp)

    barrier = pltpu.get_barrier_semaphore()
    for e in range(1, 2 * n):
        pl.semaphore_signal(barrier, inc=1, device_id=(lax.rem(i + e, 2 * n), j), device_id_type=MESH)
    for d in range(1, n):
        for cc in range(2):
            pl.semaphore_signal(barrier, inc=1, device_id=(2 * p + cc, mod(j + d)), device_id_type=MESH)
    pl.semaphore_wait(barrier, 2 * n - 1 + 2 * (n - 1))

    @pl.when(even)
    def _():
        for q in range(n // 2):
            begin[p, q] = bx_ref[q * chunk : (q + 1) * chunk, :]

    @pl.when(odd)
    def _():
        for q in range(n):
            begin[j, q] = by_ref[q * chunk : (q + 1) * chunk, :]
        for d in range(1, n):
            rc(begin.at[j, p], begin.at[j, p], bzs.at[d], bzr.at[d], (i, mod(j + d))).start()

    ykey = j * 2 + c

    def right(src, s):
        return rc(src, hw.at[s], zr.at[s], yr.at[s], (2 * p + 1, jnp.minimum(j + 1, n - 1)))

    def left(src, s):
        return rc(src, hw.at[s], zl.at[s], yr.at[s], (2 * p + 1, jnp.maximum(j - 1, 0)))

    pl.when(j < n - 1)(lambda: right(h_ref, ykey).start())
    pl.when(j > 0)(lambda: left(h_ref, ykey).start())

    def own_copy():
        return pltpu.make_async_copy(h_ref, hw.at[jnp.where(even, i, ykey)], own.at[0])

    own_copy().start()
    pl.when(even)(lambda: rc(h_ref, hw.at[ykey], ks.at[0], yr.at[ykey], sibling).start())
    pl.when(odd)(lambda: rc(h_ref, hw.at[i], ks.at[0], xr.at[i], sibling).start())

    half = n // 2

    def start_x(e):
        to = mod(p + e)
        dst = begin.at[p, pl.ds(c * half, half)]
        return rc(bxc, dst, bs.at[e], br.at[i], (2 * to, j))

    bxc = bx_ref.reshape(half, chunk, rank)

    def plane_x(e):
        return rc(h_ref, hw.at[i], xs.at[e], xr.at[i], (2 * mod(p + e), j))

    pl.when(odd)(lambda: start_x(0).start())
    for e in range(1, n):
        plane_x(e).start()
    for e in range(1, n):
        start_x(e).start()
    own_copy().wait()

    @pl.when(even)
    def _():
        rc(h_ref, hw.at[i + 1], ks.at[0], xr.at[i + 1], sibling).wait_recv()

        def cols(slot):
            for q in range(2):
                total = None
                for s in range(slabs):
                    term = bdot(hw[2 * p + q, s], hw[slot, s], NT)
                    total = term if total is None else total + term
                hi, lo = split(total)
                at = pl.ds(pl.multiple_of(slot * hrows, hrows), hrows)
                ghi[q * hrows : (q + 1) * hrows, at] = hi
                glo[q * hrows : (q + 1) * hrows, at] = lo

        cols(2 * p)
        cols(2 * p + 1)

        def step(e, carry):
            for q in range(2):
                slot = 2 * lax.rem(p - e + n, n) + q
                rc(h_ref, hw.at[slot], ks.at[0], xr.at[slot], sibling).wait_recv()
                cols(slot)
            return carry

        lax.fori_loop(1, n, step, 0)
        rc(bxc, begin.at[p, pl.ds(half, half)], ks.at[0], br.at[i + 1], sibling).wait_recv()
        for e in range(1, n):
            pp = mod(p - e)
            for q in range(2):
                rc(bxc, begin.at[pp, pl.ds(q * half, half)], ks.at[0], br.at[2 * pp + q], sibling).wait_recv()

    @pl.when(odd)
    def _():
        for d in range(1, n):
            jj = mod(j - d)
            rc(begin.at[jj, p], begin.at[jj, p], bzs.at[0], bzr.at[d], sibling).wait_recv()
            for e in range(1, n):
                rc(begin.at[jj, p], begin.at[jj, p], bps.at[e, d], bpr.at[e, d], (2 * mod(p + e) + 1, j)).start()
        rc(h_ref, hw.at[j * 2], ks.at[0], yr.at[j * 2], sibling).wait_recv()

        def cols(jj):
            total = None
            for q in range(2):
                for s in range(slabs):
                    term = bdot(hw[2 * j + q, s], hw[2 * jj + q, s], TN)
                    total = term if total is None else total + term
            hi, lo = split(total)
            at = pl.ds(pl.multiple_of(jj * hcols, hcols), hcols)
            ghi[:, at] = hi
            glo[:, at] = lo

        cols(j)

        def step(d, carry):
            for q in range(2):
                @pl.when(j - d >= 0)
                def _():
                    s = jnp.maximum(j - d, 0) * 2 + q
                    right(hw.at[s], s).wait_recv()
                    pl.when(j < n - 1)(lambda: right(hw.at[s], s).start())

                @pl.when(j + d < n)
                def _():
                    s = jnp.minimum(j + d, n - 1) * 2 + q
                    left(hw.at[s], s).wait_recv()
                    pl.when(j > 0)(lambda: left(hw.at[s], s).start())

            pl.when(j - d >= 0)(lambda: cols(jnp.maximum(j - d, 0)))
            pl.when(j + d < n)(lambda: cols(jnp.minimum(j + d, n - 1)))
            return carry

        lax.fori_loop(1, n, step, 0)
        for d in range(1, n):
            for e in range(1, n):
                at = begin.at[mod(j - d), mod(p - e)]
                rc(at, at, bzs.at[0], bpr.at[e, d], sibling).wait_recv()

    def reduce_copy(it, d):
        to = mod(r + d)
        return rc(part.at[it, to], rslots.at[it, d - 1], rs.at[it, d], rr.at[it, d], dev(a, to))

    def product(it):
        def block(to):
            at = pl.ds(pl.multiple_of(to * chunk, chunk), chunk)
            basis = bhi[...], blo[...]
            part[it, to] = dot3((ghi[at, :], glo[at, :]), basis, NN)

        for d in range(1, n):
            block(mod(r + d))
            reduce_copy(it, d).start()
        block(r)

    def spread_basis(source):
        def step(q, carry):
            at = pl.ds(pl.multiple_of(q * chunk, chunk), chunk)
            hi, lo = split(source(q // n, lax.rem(q, n)))
            bhi[at, :] = hi
            blo[at, :] = lo
            return carry

        lax.fori_loop(0, n * n, step, 0)

    spread_basis(lambda q, w: begin[q, w])
    product(0)

    def line_copy(it, d, src_j, to_j):
        q, w = place(p, src_j)
        return rc(image.at[it, q, w], image.at[it, q, w], as_.at[it, d], ar.at[it, d], (i, to_j))

    def plane_copy(it, e, d):
        q, w = place(p, mod(j - d))
        return rc(image.at[it, q, w], image.at[it, q, w], ps.at[it, e, d], pr.at[it, e, d], (2 * mod(p + e) + c, j))

    def inner_one(it, e):
        to = mod(p + e)
        return rc(ipart.at[it, to], islots.at[it, e - 1], i1s.at[it, e], i1r.at[it, e], (2 * to + c, j))

    def inner_two(it, e):
        return rc(inner.at[it, p], inner.at[it, p], i2s.at[it, e], i2r.at[it, e], (2 * mod(p + e) + c, j))

    def iteration(it, carry):
        for d in range(1, n):
            reduce_copy(it, d).wait_recv()
        total = part[it, r]
        for d in range(1, n):
            total = total + rslots[it, d - 1]
        image[it, a, r] = total
        for d in range(1, n):
            line_copy(it, d, j, mod(j + d)).start()
        square = mul(total, total, TN)
        for d in range(1, n):
            line_copy(it, d, mod(j - d), j).wait_recv()
            q, w = place(p, mod(j - d))
            rows = image[it, q, w]
            square = square + mul(rows, rows, TN)
        ipart[it] = square.reshape(n, irows, rank)
        for e in range(1, n):
            inner_one(it, e).start()
        for e in range(1, n):
            inner_one(it, e).wait_recv()
        total = ipart[it, p]
        for e in range(1, n):
            total = total + islots[it, e - 1]
        inner[it, p] = total
        for e in range(1, n):
            inner_two(it, e).start()
        for d in range(n):
            for e in range(1, n):
                plane_copy(it, e, d).start()
        for e in range(1, n):
            at = inner.at[it, mod(p - e)]
            rc(at, at, i2s.at[it, e], i2r.at[it, e], sibling).wait_recv()
        inverse_factor(inner[it].reshape(rank, rank), work, linv)
        for d in range(n):
            for e in range(1, n):
                q, w = place(mod(p - e), mod(j - d))
                at = image.at[it, q, w]
                rc(at, at, ps.at[it, e, d], pr.at[it, e, d], sibling).wait_recv()

        @pl.when(it < ITERS - 1)
        def _():
            turn = split(linv[...])
            spread_basis(lambda q, w: dot3(split(image[it, q, w]), turn, NT))
            product(jnp.minimum(it + 1, ITERS - 1))

        for d in range(1, n):
            reduce_copy(it, d).wait_send()
            line_copy(it, d, j, mod(j + d)).wait_send()
        for e in range(1, n):
            inner_one(it, e).wait_send()
            inner_two(it, e).wait_send()
            for d in range(n):
                plane_copy(it, e, d).wait_send()
        return carry

    lax.fori_loop(0, ITERS, iteration, 0)

    last = ITERS - 1
    arows, bcols = out_ref.shape[1], out_ref.shape[2]
    give = rc(fxt, fxt, fs.at[0], fr.at[0], sibling)

    @pl.when(even)
    def _():
        turn = split(linv[...])
        rows = image[last, p].reshape(n * chunk, rank)
        fxt[...] = dot3(turn, split(rows), NT).astype(BF16)
        give.start()

    def part_copy(to):
        return rc(cpart.at[to], oslots.at[p], os_.at[to], or_.at[p], (to, j))

    @pl.when(odd)
    def _():
        turn = split(linv[pl.ds(pl.multiple_of(j * bcols, bcols), bcols), :])

        def step(q, carry):
            rows = image[last, q // n, lax.rem(q, n)]
            fy[pl.ds(pl.multiple_of(q * chunk, chunk), chunk), :] = dot3(split(rows), turn, NT).astype(BF16)
            return carry

        lax.fori_loop(0, n * n, step, 0)
        for q in range(2):
            for s in range(slabs):
                total = None
                for jj in range(n):
                    term = bdot(hw[2 * jj + q, s], fy[jj * hcols : (jj + 1) * hcols, :], NN)
                    total = term if total is None else total + term
                wsum[q, s] = total
        give.wait_recv()
        for s in range(slabs):
            total = None
            for q in range(2):
                turned = fxt[:, q * hrows : (q + 1) * hrows]
                hi, lo = split(wsum[q, s])
                term = bdot(turned, hi, NN) + bdot(turned, lo, NN)
                total = term if total is None else total + term
            for to in range(2 * n):
                cpart[to, s] = total[to * arows : (to + 1) * arows, :]
        for e in range(1, 2 * n):
            part_copy(lax.rem(i + e, 2 * n)).start()
        oslots[p] = cpart[i]

    for pp in range(n):
        @pl.when(jnp.logical_or(even, p != pp))
        def _():
            rc(oslots.at[pp], oslots.at[pp], fs.at[0], or_.at[pp], sibling).wait_recv()

    total = oslots[0]
    for pp in range(1, n):
        total = total + oslots[pp]
    out_ref[...] = total

    pl.when(even)(lambda: give.wait_send())
    pl.when(even)(lambda: rc(h_ref, hw.at[ykey], ks.at[0], yr.at[ykey], sibling).wait_send())
    pl.when(odd)(lambda: rc(h_ref, hw.at[i], ks.at[0], xr.at[i], sibling).wait_send())
    pl.when(odd)(lambda: start_x(0).wait_send())
    for e in range(1, n):
        plane_x(e).wait_send()
        start_x(e).wait_send()
    pl.when(jnp.logical_and(even, j < n - 1))(lambda: right(h_ref, ykey).wait_send())
    pl.when(jnp.logical_and(even, j > 0))(lambda: left(h_ref, ykey).wait_send())

    @pl.when(odd)
    def _():
        for e in range(1, 2 * n):
            part_copy(lax.rem(i + e, 2 * n)).wait_send()
        for d in range(1, n):
            rc(begin.at[j, p], begin.at[j, p], bzs.at[d], bzr.at[d], (i, mod(j + d))).wait_send()
            for e in range(1, n):
                at = begin.at[mod(j - d), p]
                rc(at, at, bps.at[e, d], bpr.at[e, d], (2 * mod(p + e) + 1, j)).wait_send()
        for d in range(n):
            for q in range(2):
                if d == 0 and q == 0:
                    pl.when(j < n - 1)(lambda: right(h_ref, ykey).wait_send())
                    pl.when(j > 0)(lambda: left(h_ref, ykey).wait_send())
                if d == 0:
                    continue

                @pl.when(jnp.logical_and(j - d >= 0, j < n - 1))
                def _():
                    s = jnp.maximum(j - d, 0) * 2 + q
                    right(hw.at[s], s).wait_send()

                @pl.when(jnp.logical_and(j + d < n, j > 0))
                def _():
                    s = jnp.minimum(j + d, n - 1) * 2 + q
                    left(hw.at[s], s).wait_send()


def on_device(history, start_x, start_y):
    nx, n = lax.axis_size("gx"), lax.axis_size("gy")
    slabs, hrows, hcols = history.shape
    rank = start_x.shape[1]
    rows = 2 * hrows
    assert nx == 2 * n and rows == hcols and n % 2 == 0
    chunk = rows // n
    dma = pltpu.SemaphoreType.DMA
    vmem = pltpu.VMEM
    arows, bcols = rank // nx, rank // n
    shape = (slabs, arows, bcols)
    scratch = [
        vmem((2 * n, slabs, hrows, hcols), BF16),
        vmem((rows, n * rows), BF16), vmem((rows, n * rows), BF16),
        vmem((n, n, chunk, rank), F32),
        vmem((n * rows, rank), BF16), vmem((n * rows, rank), BF16),
        vmem((ITERS, n, chunk, rank), F32),
        vmem((ITERS, n - 1, chunk, rank), F32),
        vmem((ITERS, n, n, chunk, rank), F32),
        vmem((ITERS, n, rank // n, rank), F32),
        vmem((ITERS, n - 1, rank // n, rank), F32),
        vmem((ITERS, n, rank // n, rank), F32),
        vmem((rank, 2 * rank), F32),
        vmem((rank, rank), F32),
        vmem((rank, rows), BF16),
        vmem((n * rows, bcols), BF16),
        vmem((2, slabs, hrows, bcols), F32),
        vmem((nx,) + shape, F32),
        vmem((n,) + shape, F32),
        dma((1,)),
        dma((n,)), dma((nx,)),
        dma((n,)), dma((n,)),
        dma((n, n)), dma((n, n)),
        dma((n,)), dma((nx,)),
        dma((nx,)), dma((nx,)), dma((1,)), dma((nx,)),
        dma((ITERS, n)), dma((ITERS, n)),
        dma((ITERS, n)), dma((ITERS, n)),
        dma((ITERS, n, n)), dma((ITERS, n, n)),
        dma((ITERS, n)), dma((ITERS, n)),
        dma((ITERS, n)), dma((ITERS, n)),
        dma((1,)), dma((1,)),
        dma((nx,)), dma((n,)),
    ]
    return pl.pallas_call(
        functools.partial(kernel, n),
        out_shape=jax.ShapeDtypeStruct(shape, F32),
        in_specs=[pl.BlockSpec(memory_space=pltpu.VMEM)] * 3,
        out_specs=pl.BlockSpec(memory_space=pltpu.VMEM),
        scratch_shapes=scratch,
        compiler_params=pltpu.CompilerParams(
            collective_id=0, has_side_effects=True, vmem_limit_bytes=56 * 1024 * 1024
        ),
        name="tucker",
    )(history, start_x, start_y)


def solution(mesh):
    return jax.shard_map(
        on_device,
        mesh=mesh,
        in_specs=(P(None, "gx", "gy"), P("gx", None), P("gy", None)),
        out_specs=P(None, "gx", "gy"),
        check_vma=False,
    )
```

```python
import functools

import jax
import jax.numpy as jnp
from jax import lax
from jax.experimental import pallas as pl
from jax.experimental.pallas import tpu as pltpu
from jax.sharding import PartitionSpec as P

ITERS = 3
BLOCK = 64
HIGHEST = lax.Precision.HIGHEST
MESH = pl.DeviceIdType.MESH
F32, BF16 = jnp.float32, jnp.bfloat16
NN, NT, TN = ((1,), (0,)), ((1,), (1,)), ((0,), (0,))


def mul(a, b, dims):
    return lax.dot_general(a, b, (dims, ((), ())), precision=HIGHEST, preferred_element_type=F32)


def bdot(a, b, dims):
    return lax.dot_general(a, b, (dims, ((), ())), preferred_element_type=F32)


def split(v):
    hi = v.astype(BF16)
    return hi, (v - hi.astype(F32)).astype(BF16)


def dot3(a, b, dims):
    return bdot(a[0], b[0], dims) + (bdot(a[0], b[1], dims) + bdot(a[1], b[0], dims))


def eliminate(block):
    size = block.shape[0]
    sub = lax.broadcasted_iota(jnp.int32, (size, size), 0)
    lane = lax.broadcasted_iota(jnp.int32, (size, size), 1)
    eye = jnp.where(sub == lane, 1.0, 0.0).astype(F32)
    full = (8, 2 * size)
    sub8 = lax.broadcasted_iota(jnp.int32, full, 0)
    whole = jnp.concatenate([block, eye], axis=1)
    rows = [whole[t * 8 : t * 8 + 8] for t in range(size // 8)]
    for home in range(size // 8):
        k = home * 8
        tiles = range(home, size // 8)
        cols = {t: [jnp.broadcast_to(rows[t][:, k + m : k + m + 1], full) for m in range(8)] for t in tiles}
        piv = [[jnp.broadcast_to(cols[home][l][m : m + 1, :], full) for l in range(8)] for m in range(8)]
        held = [jnp.broadcast_to(rows[home][m : m + 1, :], full) for m in range(8)]
        inv = []
        for m in range(0, 8, 2):
            first, cross, second = piv[m][m], piv[m][m + 1], piv[m + 1][m + 1]
            inv0 = 1.0 / first
            inv1 = first * (1.0 / (first * second - cross * cross))
            ratio = cross * inv0
            inv += [inv0, inv1]
            held[m + 1] = held[m + 1] - ratio * held[m]
            for t in tiles:
                cols[t][m + 1] = cols[t][m + 1] - ratio * cols[t][m]
            for l in range(m + 2, 8):
                piv[m + 1][l] = piv[m + 1][l] - ratio * piv[m][l]
            for q in range(m + 2, 8):
                by0, by1 = piv[m][q] * inv0, piv[m + 1][q] * inv1
                for l in range(q, 8):
                    piv[q][l] = piv[q][l] - by0 * piv[m][l] - by1 * piv[m + 1][l]
                held[q] = held[q] - by0 * held[m] - by1 * held[m + 1]
                for t in tiles:
                    cols[t][q] = cols[t][q] - by0 * cols[t][m] - by1 * cols[t][m + 1]
        scaled = [held[m] * inv[m] for m in range(8)]
        for t in tiles:
            for m in range(8):
                col = cols[t][m]
                if t == home:
                    if m == 7:
                        continue
                    col = jnp.where(sub8 > m, col, 0.0)
                rows[t] = rows[t] - col * scaled[m]
    whole = jnp.concatenate(rows, axis=0)
    diag = jnp.sum(jnp.where(sub == lane, whole[:, :size], 0.0), axis=1, keepdims=True)
    return whole[:, size:] * (1.0 / jnp.sqrt(diag))


def inverse_factor(inner, work, out_ref, between):
    rank = inner.shape[0]
    sub = lax.broadcasted_iota(jnp.int32, (rank, rank), 0)
    lane = lax.broadcasted_iota(jnp.int32, (rank, rank), 1)
    same = sub == lane
    diag = jnp.where(same, inner, 0.0)
    tall = 1.0 / jnp.sqrt(jnp.sum(diag, axis=1, keepdims=True))
    wide = 1.0 / jnp.sqrt(jnp.sum(diag, axis=0, keepdims=True))
    work[:, :rank] = inner * tall * wide
    work[:, rank:] = jnp.where(same, 1.0, 0.0).astype(F32)
    for step, at in enumerate(range(0, rank, BLOCK)):
        inverse = eliminate(work[at : at + BLOCK, at : at + BLOCK])
        top = mul(inverse, work[at : at + BLOCK, :], NN)
        out_ref[at : at + BLOCK, :] = top[:, rank:] * wide
        if at + BLOCK < rank:
            left = top[:, at + BLOCK : rank]
            work[at + BLOCK :, :] = work[at + BLOCK :, :] - mul(left, top, TN)
        between(step, rank // BLOCK)


def kernel(
    n, h_ref, bx_ref, by_ref, out_ref,
    hw, ghi, glo, begin, bhi, blo, part, rslots, image, ipart, islots, inner, work, linv, fxt, fy, wsum, cpart, oslots,
    own, bs, br, bzs, bzr, bps, bpr, xs, xr, zr, zl, ks, yr, rs, rr, as_, ar, ps, pr, i1s, i1r, i2s, i2r, fs, fr, os_, or_,
):
    i, j = lax.axis_index("gx"), lax.axis_index("gy")
    p, c = i // 2, lax.rem(i, 2)
    even = c == 0
    odd = c == 1
    slabs, hrows, hcols = h_ref.shape
    rank = bx_ref.shape[1]
    chunk = image.shape[3]
    irows = rank // n
    sibling = (i + 1 - 2 * c, j)

    def mod(v):
        return lax.rem(v + n, n)

    def rc(src, dst, ss, rsem, dev):
        return pltpu.make_async_remote_copy(
            src_ref=src, dst_ref=dst, send_sem=ss, recv_sem=rsem, device_id=dev, device_id_type=MESH
        )

    a = jnp.where(even, p, j)
    r = jnp.where(even, j, p)

    def dev(aa, rr_):
        return (jnp.where(even, 2 * aa, 2 * rr_ + 1), jnp.where(even, rr_, aa))

    def place(pp, jj):
        return jnp.where(even, pp, jj), jnp.where(even, jj, pp)

    barrier = pltpu.get_barrier_semaphore()
    for e in range(1, 2 * n):
        pl.semaphore_signal(barrier, inc=1, device_id=(lax.rem(i + e, 2 * n), j), device_id_type=MESH)
    for d in range(1, n):
        for cc in range(2):
            pl.semaphore_signal(barrier, inc=1, device_id=(2 * p + cc, mod(j + d)), device_id_type=MESH)
    pl.semaphore_wait(barrier, 2 * n - 1 + 2 * (n - 1))

    @pl.when(even)
    def _():
        for q in range(n // 2):
            begin[p, q] = bx_ref[q * chunk : (q + 1) * chunk, :]

    @pl.when(odd)
    def _():
        for q in range(n):
            begin[j, q] = by_ref[q * chunk : (q + 1) * chunk, :]
        for d in range(1, n):
            rc(begin.at[j, p], begin.at[j, p], bzs.at[d], bzr.at[d], (i, mod(j + d))).start()

    ykey = j * 2 + c

    def right(src, s):
        return rc(src, hw.at[s], zr.at[s], yr.at[s], (2 * p + 1, jnp.minimum(j + 1, n - 1)))

    def left(src, s):
        return rc(src, hw.at[s], zl.at[s], yr.at[s], (2 * p + 1, jnp.maximum(j - 1, 0)))

    pl.when(j < n - 1)(lambda: right(h_ref, ykey).start())
    pl.when(j > 0)(lambda: left(h_ref, ykey).start())

    def own_copy():
        return pltpu.make_async_copy(h_ref, hw.at[jnp.where(even, i, ykey)], own.at[0])

    own_copy().start()
    pl.when(even)(lambda: rc(h_ref, hw.at[ykey], ks.at[0], yr.at[ykey], sibling).start())
    pl.when(odd)(lambda: rc(h_ref, hw.at[i], ks.at[0], xr.at[i], sibling).start())

    half = n // 2

    def start_x(e):
        to = mod(p + e)
        dst = begin.at[p, pl.ds(c * half, half)]
        return rc(bxc, dst, bs.at[e], br.at[i], (2 * to, j))

    bxc = bx_ref.reshape(half, chunk, rank)

    def plane_x(e):
        return rc(h_ref, hw.at[i], xs.at[e], xr.at[i], (2 * mod(p + e), j))

    pl.when(odd)(lambda: start_x(0).start())
    for e in range(1, n):
        plane_x(e).start()
    for e in range(1, n):
        start_x(e).start()
    own_copy().wait()

    @pl.when(even)
    def _():
        rc(h_ref, hw.at[i + 1], ks.at[0], xr.at[i + 1], sibling).wait_recv()

        def cols(slot):
            for q in range(2):
                total = None
                for s in range(slabs):
                    term = bdot(hw[2 * p + q, s], hw[slot, s], NT)
                    total = term if total is None else total + term
                hi, lo = split(total)
                at = pl.ds(pl.multiple_of(slot * hrows, hrows), hrows)
                ghi[q * hrows : (q + 1) * hrows, at] = hi
                glo[q * hrows : (q + 1) * hrows, at] = lo

        cols(2 * p)
        cols(2 * p + 1)

        def step(e, carry):
            for q in range(2):
                slot = 2 * lax.rem(p - e + n, n) + q
                rc(h_ref, hw.at[slot], ks.at[0], xr.at[slot], sibling).wait_recv()
                cols(slot)
            return carry

        lax.fori_loop(1, n, step, 0)
        rc(bxc, begin.at[p, pl.ds(half, half)], ks.at[0], br.at[i + 1], sibling).wait_recv()
        for e in range(1, n):
            pp = mod(p - e)
            for q in range(2):
                rc(bxc, begin.at[pp, pl.ds(q * half, half)], ks.at[0], br.at[2 * pp + q], sibling).wait_recv()

    @pl.when(odd)
    def _():
        for d in range(1, n):
            jj = mod(j - d)
            rc(begin.at[jj, p], begin.at[jj, p], bzs.at[0], bzr.at[d], sibling).wait_recv()
            for e in range(1, n):
                rc(begin.at[jj, p], begin.at[jj, p], bps.at[e, d], bpr.at[e, d], (2 * mod(p + e) + 1, j)).start()
        rc(h_ref, hw.at[j * 2], ks.at[0], yr.at[j * 2], sibling).wait_recv()

        def cols(jj):
            total = None
            for q in range(2):
                for s in range(slabs):
                    term = bdot(hw[2 * j + q, s], hw[2 * jj + q, s], TN)
                    total = term if total is None else total + term
            hi, lo = split(total)
            at = pl.ds(pl.multiple_of(jj * hcols, hcols), hcols)
            ghi[:, at] = hi
            glo[:, at] = lo

        cols(j)

        def step(d, carry):
            for q in range(2):
                @pl.when(j - d >= 0)
                def _():
                    s = jnp.maximum(j - d, 0) * 2 + q
                    right(hw.at[s], s).wait_recv()
                    pl.when(j < n - 1)(lambda: right(hw.at[s], s).start())

                @pl.when(j + d < n)
                def _():
                    s = jnp.minimum(j + d, n - 1) * 2 + q
                    left(hw.at[s], s).wait_recv()
                    pl.when(j > 0)(lambda: left(hw.at[s], s).start())

            pl.when(j - d >= 0)(lambda: cols(jnp.maximum(j - d, 0)))
            pl.when(j + d < n)(lambda: cols(jnp.minimum(j + d, n - 1)))
            return carry

        lax.fori_loop(1, n, step, 0)
        for d in range(1, n):
            for e in range(1, n):
                at = begin.at[mod(j - d), mod(p - e)]
                rc(at, at, bzs.at[0], bpr.at[e, d], sibling).wait_recv()

    def reduce_copy(it, d):
        to = mod(r + d)
        return rc(part.at[it, to], rslots.at[it, d - 1], rs.at[it, d], rr.at[it, d], dev(a, to))

    def product(it):
        def block(to):
            at = pl.ds(pl.multiple_of(to * chunk, chunk), chunk)
            basis = bhi[...], blo[...]
            part[it, to] = dot3((ghi[at, :], glo[at, :]), basis, NN)

        for d in range(1, n):
            block(mod(r + d))
            reduce_copy(it, d).start()
        block(r)

    def spread_basis(source):
        def step(q, carry):
            at = pl.ds(pl.multiple_of(q * n * chunk, n * chunk), n * chunk)
            hi, lo = split(source(q).reshape(n * chunk, rank))
            bhi[at, :] = hi
            blo[at, :] = lo
            return carry

        lax.fori_loop(0, n, step, 0)

    def turned(it, turn):
        return lambda q: dot3(split(image[it, q].reshape(n * chunk, rank)), turn, NT)

    spread_basis(lambda q: begin[q])
    product(0)

    def line_copy(it, d, src_j, to_j):
        q, w = place(p, src_j)
        return rc(image.at[it, q, w], image.at[it, q, w], as_.at[it, d], ar.at[it, d], (i, to_j))

    corner = n == 4
    hops = (1, 2) if corner else tuple(range(1, n))
    far = (3,) if corner else hops

    def across(e):
        return (p + 1 - 2 * lax.rem(p, 2), lax.rem(p + 2, n), n - 1 - p)[e - 1]

    def peer(e):
        return across(e) if corner else mod(p + e)

    def source(e):
        return across(e) if corner else mod(p - e)

    def plane_copy(it, e, d):
        q, w = place(p, mod(j - d))
        return rc(image.at[it, q, w], image.at[it, q, w], ps.at[it, e, d], pr.at[it, e, d], (2 * peer(e) + c, j))

    def half_copy(it, e, d):
        q, w = place(source(e), mod(j - d))
        at = image.at[it, q, w, pl.ds((e - 1) * (chunk // 2), chunk // 2)]
        return rc(at, at, ps.at[it, 0 if e == 1 else 3, d], pr.at[it, 0 if e == 1 else 3, d], (2 * peer(3 - e) + c, j))

    def forward(it, d):
        if corner:
            for e in hops:
                q, w = place(source(e), mod(j - d))
                at = image.at[it, q, w]
                rc(at, at, ps.at[it, e, d], pr.at[it, e, d], sibling).wait_recv()
                half_copy(it, e, d).start()

    def arriving(it, e, d):
        q, w = place(source(e), mod(j - d))
        if not corner:
            return [(image.at[it, q, w], ps.at[it, e, d], pr.at[it, e, d])]
        return [
            (image.at[it, q, w, pl.ds(b * (chunk // 2), chunk // 2)], ps.at[it, 3 * b, d], pr.at[it, 3 * b, d])
            for b in range(2)
        ]

    def inner_one(it, e):
        to = mod(p + e)
        return rc(ipart.at[it, to], islots.at[it, e - 1], i1s.at[it, e], i1r.at[it, e], (2 * to + c, j))

    def inner_two(it, e):
        return rc(inner.at[it, p], inner.at[it, p], i2s.at[it, e], i2r.at[it, e], (2 * mod(p + e) + c, j))

    def iteration(it, carry):
        for d in range(1, n):
            reduce_copy(it, d).wait_recv()
        total = part[it, r]
        for d in range(1, n):
            total = total + rslots[it, d - 1]
        image[it, a, r] = total
        for d in range(1, n):
            line_copy(it, d, j, mod(j + d)).start()
        square = mul(total, total, TN)
        for d in range(1, n):
            line_copy(it, d, mod(j - d), j).wait_recv()
            q, w = place(p, mod(j - d))
            rows = image[it, q, w]
            square = square + mul(rows, rows, TN)
        ipart[it] = square.reshape(n, irows, rank)
        for e in range(1, n):
            inner_one(it, e).start()
        for e in range(1, n):
            inner_one(it, e).wait_recv()
        total = ipart[it, p]
        for e in range(1, n):
            total = total + islots[it, e - 1]
        inner[it, p] = total
        for e in range(1, n):
            inner_two(it, e).start()
        spread_needed = jnp.logical_or(odd, it < ITERS - 1)

        @pl.when(spread_needed)
        def _():
            for d in range(n):
                for e in hops:
                    plane_copy(it, e, d).start()

        for e in range(1, n):
            at = inner.at[it, mod(p - e)]
            rc(at, at, i2s.at[it, e], i2r.at[it, e], sibling).wait_recv()

        def between(step, steps):
            for d in range(n):
                if min(d, steps - 1) == step:
                    pl.when(spread_needed)(lambda: forward(it, d))

        inverse_factor(inner[it].reshape(rank, rank), work, linv, between)

        @pl.when(spread_needed)
        def _():
            for d in range(n):
                for e in far:
                    for at in arriving(it, e, d):
                        rc(at[0], at[0], at[1], at[2], sibling).wait_recv()


        @pl.when(it < ITERS - 1)
        def _():
            turn = split(linv[...])
            spread_basis(turned(it, turn))
            product(jnp.minimum(it + 1, ITERS - 1))

        for d in range(1, n):
            reduce_copy(it, d).wait_send()
            line_copy(it, d, j, mod(j + d)).wait_send()
        for e in range(1, n):
            inner_one(it, e).wait_send()
            inner_two(it, e).wait_send()

        @pl.when(spread_needed)
        def _():
            for d in range(n):
                for e in hops:
                    plane_copy(it, e, d).wait_send()
                    if corner:
                        half_copy(it, e, d).wait_send()

        return carry

    lax.fori_loop(0, ITERS, iteration, 0)

    last = ITERS - 1
    arows, bcols = out_ref.shape[1], out_ref.shape[2]
    give = rc(fxt, fxt, fs.at[0], fr.at[0], sibling)

    @pl.when(even)
    def _():
        turn = split(linv[...])
        rows = image[last, p].reshape(n * chunk, rank)
        fxt[...] = dot3(turn, split(rows), NT).astype(BF16)
        give.start()

    def part_copy(to):
        return rc(cpart.at[to], oslots.at[p], os_.at[to], or_.at[p], (to, j))

    @pl.when(odd)
    def _():
        turn = split(linv[pl.ds(pl.multiple_of(j * bcols, bcols), bcols), :])

        def step(q, carry):
            at = pl.ds(pl.multiple_of(q * n * chunk, n * chunk), n * chunk)
            fy[at, :] = turned(last, turn)(q).astype(BF16)
            return carry

        lax.fori_loop(0, n, step, 0)
        for q in range(2):
            for s in range(slabs):
                total = None
                for jj in range(n):
                    term = bdot(hw[2 * jj + q, s], fy[jj * hcols : (jj + 1) * hcols, :], NN)
                    total = term if total is None else total + term
                wsum[q, s] = total
        give.wait_recv()
        for s in range(slabs):
            total = None
            for q in range(2):
                tall = fxt[:, q * hrows : (q + 1) * hrows]
                hi, lo = split(wsum[q, s])
                term = bdot(tall, hi, NN) + bdot(tall, lo, NN)
                total = term if total is None else total + term
            for to in range(2 * n):
                cpart[to, s] = total[to * arows : (to + 1) * arows, :]
        for e in range(1, 2 * n):
            part_copy(lax.rem(i + e, 2 * n)).start()
        oslots[p] = cpart[i]

    for pp in range(n):
        @pl.when(jnp.logical_or(even, p != pp))
        def _():
            rc(oslots.at[pp], oslots.at[pp], fs.at[0], or_.at[pp], sibling).wait_recv()

    total = oslots[0]
    for pp in range(1, n):
        total = total + oslots[pp]
    out_ref[...] = total

    pl.when(even)(lambda: give.wait_send())
    pl.when(even)(lambda: rc(h_ref, hw.at[ykey], ks.at[0], yr.at[ykey], sibling).wait_send())
    pl.when(odd)(lambda: rc(h_ref, hw.at[i], ks.at[0], xr.at[i], sibling).wait_send())
    pl.when(odd)(lambda: start_x(0).wait_send())
    for e in range(1, n):
        plane_x(e).wait_send()
        start_x(e).wait_send()
    pl.when(jnp.logical_and(even, j < n - 1))(lambda: right(h_ref, ykey).wait_send())
    pl.when(jnp.logical_and(even, j > 0))(lambda: left(h_ref, ykey).wait_send())

    @pl.when(odd)
    def _():
        for e in range(1, 2 * n):
            part_copy(lax.rem(i + e, 2 * n)).wait_send()
        for d in range(1, n):
            rc(begin.at[j, p], begin.at[j, p], bzs.at[d], bzr.at[d], (i, mod(j + d))).wait_send()
            for e in range(1, n):
                at = begin.at[mod(j - d), p]
                rc(at, at, bps.at[e, d], bpr.at[e, d], (2 * mod(p + e) + 1, j)).wait_send()
        for d in range(n):
            for q in range(2):
                if d == 0 and q == 0:
                    pl.when(j < n - 1)(lambda: right(h_ref, ykey).wait_send())
                    pl.when(j > 0)(lambda: left(h_ref, ykey).wait_send())
                if d == 0:
                    continue

                @pl.when(jnp.logical_and(j - d >= 0, j < n - 1))
                def _():
                    s = jnp.maximum(j - d, 0) * 2 + q
                    right(hw.at[s], s).wait_send()

                @pl.when(jnp.logical_and(j + d < n, j > 0))
                def _():
                    s = jnp.minimum(j + d, n - 1) * 2 + q
                    left(hw.at[s], s).wait_send()


def on_device(history, start_x, start_y):
    nx, n = lax.axis_size("gx"), lax.axis_size("gy")
    slabs, hrows, hcols = history.shape
    rank = start_x.shape[1]
    rows = 2 * hrows
    assert nx == 2 * n and rows == hcols and n % 2 == 0
    chunk = rows // n
    dma = pltpu.SemaphoreType.DMA
    vmem = pltpu.VMEM
    arows, bcols = rank // nx, rank // n
    shape = (slabs, arows, bcols)
    scratch = [
        vmem((2 * n, slabs, hrows, hcols), BF16),
        vmem((rows, n * rows), BF16), vmem((rows, n * rows), BF16),
        vmem((n, n, chunk, rank), F32),
        vmem((n * rows, rank), BF16), vmem((n * rows, rank), BF16),
        vmem((ITERS, n, chunk, rank), F32),
        vmem((ITERS, n - 1, chunk, rank), F32),
        vmem((ITERS, n, n, chunk, rank), F32),
        vmem((ITERS, n, rank // n, rank), F32),
        vmem((ITERS, n - 1, rank // n, rank), F32),
        vmem((ITERS, n, rank // n, rank), F32),
        vmem((rank, 2 * rank), F32),
        vmem((rank, rank), F32),
        vmem((rank, rows), BF16),
        vmem((n * rows, bcols), BF16),
        vmem((2, slabs, hrows, bcols), F32),
        vmem((nx,) + shape, F32),
        vmem((n,) + shape, F32),
        dma((1,)),
        dma((n,)), dma((nx,)),
        dma((n,)), dma((n,)),
        dma((n, n)), dma((n, n)),
        dma((n,)), dma((nx,)),
        dma((nx,)), dma((nx,)), dma((1,)), dma((nx,)),
        dma((ITERS, n)), dma((ITERS, n)),
        dma((ITERS, n)), dma((ITERS, n)),
        dma((ITERS, n, n)), dma((ITERS, n, n)),
        dma((ITERS, n)), dma((ITERS, n)),
        dma((ITERS, n)), dma((ITERS, n)),
        dma((1,)), dma((1,)),
        dma((nx,)), dma((n,)),
    ]
    return pl.pallas_call(
        functools.partial(kernel, n),
        out_shape=jax.ShapeDtypeStruct(shape, F32),
        in_specs=[pl.BlockSpec(memory_space=pltpu.VMEM)] * 3,
        out_specs=pl.BlockSpec(memory_space=pltpu.VMEM),
        scratch_shapes=scratch,
        compiler_params=pltpu.CompilerParams(
            collective_id=0, has_side_effects=True, vmem_limit_bytes=56 * 1024 * 1024
        ),
        name="tucker",
    )(history, start_x, start_y)


def solution(mesh):
    return jax.shard_map(
        on_device,
        mesh=mesh,
        in_specs=(P(None, "gx", "gy"), P("gx", None), P("gy", None)),
        out_specs=P(None, "gx", "gy"),
        check_vma=False,
    )
```

```python
import functools

import jax
import jax.numpy as jnp
from jax import lax
from jax.experimental import pallas as pl
from jax.experimental.pallas import tpu as pltpu
from jax.sharding import PartitionSpec as P

ITERS = 3
BLOCK = 64
HIGHEST = lax.Precision.HIGHEST
MESH = pl.DeviceIdType.MESH
F32, BF16 = jnp.float32, jnp.bfloat16
NN, NT, TN = ((1,), (0,)), ((1,), (1,)), ((0,), (0,))


def mul(a, b, dims):
    return lax.dot_general(a, b, (dims, ((), ())), precision=HIGHEST, preferred_element_type=F32)


def bdot(a, b, dims):
    return lax.dot_general(a, b, (dims, ((), ())), preferred_element_type=F32)


def split(v):
    hi = v.astype(BF16)
    return hi, (v - hi.astype(F32)).astype(BF16)


def dot3(a, b, dims):
    return bdot(a[0], b[0], dims) + (bdot(a[0], b[1], dims) + bdot(a[1], b[0], dims))


def eliminate(block):
    size = block.shape[0]
    sub = lax.broadcasted_iota(jnp.int32, (size, size), 0)
    lane = lax.broadcasted_iota(jnp.int32, (size, size), 1)
    eye = jnp.where(sub == lane, 1.0, 0.0).astype(F32)
    full = (8, 2 * size)
    sub8 = lax.broadcasted_iota(jnp.int32, full, 0)
    whole = jnp.concatenate([block, eye], axis=1)
    rows = [whole[t * 8 : t * 8 + 8] for t in range(size // 8)]
    for home in range(size // 8):
        k = home * 8
        tiles = range(home, size // 8)
        cols = {t: [jnp.broadcast_to(rows[t][:, k + m : k + m + 1], full) for m in range(8)] for t in tiles}
        piv = [[jnp.broadcast_to(cols[home][l][m : m + 1, :], full) for l in range(8)] for m in range(8)]
        held = [jnp.broadcast_to(rows[home][m : m + 1, :], full) for m in range(8)]
        inv = []
        for m in range(0, 8, 2):
            first, cross, second = piv[m][m], piv[m][m + 1], piv[m + 1][m + 1]
            inv0 = 1.0 / first
            inv1 = first * (1.0 / (first * second - cross * cross))
            ratio = cross * inv0
            inv += [inv0, inv1]
            held[m + 1] = held[m + 1] - ratio * held[m]
            for t in tiles:
                cols[t][m + 1] = cols[t][m + 1] - ratio * cols[t][m]
            for l in range(m + 2, 8):
                piv[m + 1][l] = piv[m + 1][l] - ratio * piv[m][l]
            for q in range(m + 2, 8):
                by0, by1 = piv[m][q] * inv0, piv[m + 1][q] * inv1
                for l in range(q, 8):
                    piv[q][l] = piv[q][l] - by0 * piv[m][l] - by1 * piv[m + 1][l]
                held[q] = held[q] - by0 * held[m] - by1 * held[m + 1]
                for t in tiles:
                    cols[t][q] = cols[t][q] - by0 * cols[t][m] - by1 * cols[t][m + 1]
        scaled = [held[m] * inv[m] for m in range(8)]
        for t in tiles:
            for m in range(8):
                col = cols[t][m]
                if t == home:
                    if m == 7:
                        continue
                    col = jnp.where(sub8 > m, col, 0.0)
                rows[t] = rows[t] - col * scaled[m]
    whole = jnp.concatenate(rows, axis=0)
    diag = jnp.sum(jnp.where(sub == lane, whole[:, :size], 0.0), axis=1, keepdims=True)
    return whole[:, size:] * (1.0 / jnp.sqrt(diag))


def inverse_factor(inner, work, out_ref, between):
    rank = inner.shape[0]
    sub = lax.broadcasted_iota(jnp.int32, (rank, rank), 0)
    lane = lax.broadcasted_iota(jnp.int32, (rank, rank), 1)
    same = sub == lane
    diag = jnp.where(same, inner, 0.0)
    tall = 1.0 / jnp.sqrt(jnp.sum(diag, axis=1, keepdims=True))
    wide = 1.0 / jnp.sqrt(jnp.sum(diag, axis=0, keepdims=True))
    work[:, :rank] = inner * tall * wide
    work[:, rank:] = jnp.where(same, 1.0, 0.0).astype(F32)
    for step, at in enumerate(range(0, rank, BLOCK)):
        inverse = eliminate(work[at : at + BLOCK, at : at + BLOCK])
        top = mul(inverse, work[at : at + BLOCK, :], NN)
        out_ref[at : at + BLOCK, :] = top[:, rank:] * wide
        if at + BLOCK < rank:
            left = top[:, at + BLOCK : rank]
            work[at + BLOCK :, :] = work[at + BLOCK :, :] - mul(left, top, TN)
        between(step, rank // BLOCK)


def kernel(
    n, h_ref, bx_ref, by_ref, out_ref,
    hw, ghi, glo, begin, bhi, blo, part, rslots, image, ipart, islots, inner, work, linv, fxt, fy, wsum, cpart, oslots, back_hi, back_lo, extra, final,
    own, bs, br, bzs, bzr, bps, bpr, xs, xr, zr, zl, ks, yr, rs, rr, as_, ar, ps, pr, i1s, i1r, i2s, i2r, fs, fr, os_, or_, fxs, fbs, gs, gr, es, er,
):
    i, j = lax.axis_index("gx"), lax.axis_index("gy")
    p, c = i // 2, lax.rem(i, 2)
    even = c == 0
    odd = c == 1
    slabs, hrows, hcols = h_ref.shape
    rank = bx_ref.shape[1]
    chunk = image.shape[3]
    irows = rank // n
    sibling = (i + 1 - 2 * c, j)

    def mod(v):
        return lax.rem(v + n, n)

    def rc(src, dst, ss, rsem, dev):
        return pltpu.make_async_remote_copy(
            src_ref=src, dst_ref=dst, send_sem=ss, recv_sem=rsem, device_id=dev, device_id_type=MESH
        )

    a = jnp.where(even, p, j)
    r = jnp.where(even, j, p)

    def dev(aa, rr_):
        return (jnp.where(even, 2 * aa, 2 * rr_ + 1), jnp.where(even, rr_, aa))

    def place(pp, jj):
        return jnp.where(even, pp, jj), jnp.where(even, jj, pp)

    corner = n == 4
    hops = (1, 2) if corner else tuple(range(1, n))
    far = (3,) if corner else hops

    def across(e):
        return (p + 1 - 2 * lax.rem(p, 2), lax.rem(p + 2, n), n - 1 - p)[e - 1]

    def peer(e):
        return across(e) if corner else mod(p + e)

    def source(e):
        return across(e) if corner else mod(p - e)

    barrier = pltpu.get_barrier_semaphore()
    for e in range(1, 2 * n):
        pl.semaphore_signal(barrier, inc=1, device_id=(lax.rem(i + e, 2 * n), j), device_id_type=MESH)
    for d in range(1, n):
        for cc in range(2):
            pl.semaphore_signal(barrier, inc=1, device_id=(2 * p + cc, mod(j + d)), device_id_type=MESH)
    pl.semaphore_wait(barrier, 2 * n - 1 + 2 * (n - 1))

    @pl.when(even)
    def _():
        for q in range(n // 2):
            begin[p, q] = bx_ref[q * chunk : (q + 1) * chunk, :]

    @pl.when(odd)
    def _():
        for q in range(n):
            begin[j, q] = by_ref[q * chunk : (q + 1) * chunk, :]
        for d in range(1, n):
            rc(begin.at[j, p], begin.at[j, p], bzs.at[d], bzr.at[d], (i, mod(j + d))).start()

    ykey = j * 2 + c

    width = hcols // 2
    pieces = [pl.ds(b * width, width) for b in range(2)]

    def right(src, s, b):
        to = (2 * p + 1, jnp.minimum(j + 1, n - 1))
        return rc(src.at[:, :, pieces[b]], hw.at[s, :, :, pieces[b]], zr.at[s, b], yr.at[s, b], to)

    def left(src, s, b):
        to = (2 * p + 1, jnp.maximum(j - 1, 0))
        return rc(src.at[:, :, pieces[b]], hw.at[s, :, :, pieces[b]], zl.at[s, b], yr.at[s, b], to)

    for b in range(2):
        pl.when(j < n - 1)(lambda: right(h_ref, ykey, b).start())
        pl.when(j > 0)(lambda: left(h_ref, ykey, b).start())

    def own_copy():
        return pltpu.make_async_copy(h_ref, hw.at[jnp.where(even, i, ykey)], own.at[0])

    own_copy().start()
    pl.when(even)(lambda: rc(h_ref, hw.at[ykey], ks.at[0], yr.at[ykey, 0], sibling).start())
    pl.when(odd)(lambda: rc(h_ref, hw.at[i], ks.at[0], xr.at[i, 0], sibling).start())

    half = n // 2

    bxc = bx_ref.reshape(half, chunk, rank)

    def start_x(e):
        dst = begin.at[p, pl.ds(c * half, half)]
        return rc(bxc, dst, bs.at[e], br.at[i, 0], (2 * (p if e == 0 else peer(e)), j))

    def plane_x(e):
        return rc(h_ref, hw.at[i], xs.at[e], xr.at[i, 0], (2 * peer(e), j))

    sh = slabs // 2

    def forward_x(e, q):
        slot = 2 * source(e) + q
        at = hw.at[slot, pl.ds((e - 1) * sh, sh)]
        return rc(at, at, fxs.at[e, q], xr.at[slot, e - 1], (2 * peer(3 - e), j))

    def forward_start(e, q):
        at = begin.at[source(e), q * half + e - 1]
        return rc(at, at, fbs.at[e, q], br.at[2 * source(e) + q, e - 1], (2 * peer(3 - e), j))

    pl.when(odd)(lambda: start_x(0).start())
    for e in hops:
        plane_x(e).start()
    for e in hops:
        start_x(e).start()
    own_copy().wait()

    @pl.when(even)
    def _():
        rc(h_ref, hw.at[i + 1], ks.at[0], xr.at[i + 1, 0], sibling).wait_recv()

        def cols(slot):
            for q in range(2):
                total = None
                for s in range(slabs):
                    term = bdot(hw[2 * p + q, s], hw[slot, s], NT)
                    total = term if total is None else total + term
                hi, lo = split(total)
                at = pl.ds(pl.multiple_of(slot * hrows, hrows), hrows)
                ghi[q * hrows : (q + 1) * hrows, at] = hi
                glo[q * hrows : (q + 1) * hrows, at] = lo

        def all_cols(slots):
            def step(t, carry):
                slot = slots[0]
                for u in range(1, len(slots)):
                    slot = jnp.where(t == u, slots[u], slot)
                cols(slot)
                return carry

            lax.fori_loop(0, len(slots), step, 0)

        for e in hops:
            for q in range(2):
                slot = 2 * source(e) + q
                rc(h_ref, hw.at[slot], ks.at[0], xr.at[slot, 0], sibling).wait_recv()
                if corner:
                    forward_x(e, q).start()
        all_cols([2 * p, 2 * p + 1] + [2 * source(e) + q for e in hops for q in range(2)])
        rc(bxc, begin.at[p, pl.ds(half, half)], ks.at[0], br.at[i + 1, 0], sibling).wait_recv()
        for e in hops:
            for q in range(2):
                pp = source(e)
                rc(bxc, begin.at[pp, pl.ds(q * half, half)], ks.at[0], br.at[2 * pp + q, 0], sibling).wait_recv()
                if corner:
                    forward_start(e, q).start()
        if corner:
            for q in range(2):
                slot = 2 * source(3) + q
                for b in range(2):
                    at = hw.at[slot, pl.ds(b * sh, sh)]
                    rc(at, at, ks.at[0], xr.at[slot, b], sibling).wait_recv()
            all_cols([2 * source(3), 2 * source(3) + 1])
            for q in range(2):
                for b in range(2):
                    at = begin.at[source(3), q * half + b]
                    rc(at, at, ks.at[0], br.at[2 * source(3) + q, b], sibling).wait_recv()

    def taken(s, first, last):
        return jnp.logical_or(jnp.logical_and(j == first, s > 1), jnp.logical_and(j == last, s < n - 2))

    def back_copies(to, s, b):
        at = pl.ds(pl.multiple_of(s * hcols + b * width, width), width)
        return [
            rc(src.at[s, :, pieces[b]], dst.at[:, at], gs.at[m, s, b], gr.at[m, s, b], (i, to))
            for m, (src, dst) in enumerate(((back_hi, ghi), (back_lo, glo)))
        ]

    @pl.when(odd)
    def _():
        for d in range(1, n):
            jj = mod(j - d)
            rc(begin.at[jj, p], begin.at[jj, p], bzs.at[0], bzr.at[d], sibling).wait_recv()
            for e in range(1, n):
                rc(begin.at[jj, p], begin.at[jj, p], bps.at[e, d], bpr.at[e, d], (2 * mod(p + e) + 1, j)).start()
        rc(h_ref, hw.at[j * 2], ks.at[0], yr.at[j * 2, 0], sibling).wait_recv()

        def cols(jj):
            total = None
            for q in range(2):
                for s in range(slabs):
                    term = bdot(hw[2 * j + q, s], hw[2 * jj + q, s], TN)
                    total = term if total is None else total + term
            hi, lo = split(total)
            at = pl.ds(pl.multiple_of(jj * hcols, hcols), hcols)
            ghi[:, at] = hi
            glo[:, at] = lo

        cols(j)

        def give_back(base, s, b):
            total = None
            for q in range(2):
                for t in range(slabs):
                    term = bdot(hw[2 * base + q, t], hw[2 * s + q, t, :, pieces[b]], TN)
                    total = term if total is None else total + term
            back_hi[s, :, pieces[b]], back_lo[s, :, pieces[b]] = split(total)
            for copy in back_copies(base, s, b):
                copy.start()

        def step(d, carry):
            low, high = jnp.maximum(j - d, 0), jnp.minimum(j + d, n - 1)
            from_low = jnp.logical_and(j - d >= 0, jnp.logical_or(d == 1, j < n - 1))
            from_high = jnp.logical_and(j + d < n, jnp.logical_or(d == 1, j > 0))
            for_first = jnp.logical_and(from_high, j == 1)
            for_last = jnp.logical_and(from_low, j == n - 2)
            for b in range(2):
                for q in range(2):
                    @pl.when(from_low)
                    def _():
                        s = low * 2 + q
                        right(hw.at[s], s, b).wait_recv()
                        pl.when(j < n - 2)(lambda: right(hw.at[s], s, b).start())

                    @pl.when(from_high)
                    def _():
                        s = high * 2 + q
                        left(hw.at[s], s, b).wait_recv()
                        pl.when(j > 1)(lambda: left(hw.at[s], s, b).start())

                pl.when(jnp.logical_and(for_first, d > 1))(lambda: give_back(0, high, b))
                pl.when(jnp.logical_and(for_last, d > 1))(lambda: give_back(n - 1, low, b))
            for b in range(2):
                pl.when(jnp.logical_and(for_first, d == 1))(lambda: give_back(0, high, b))
                pl.when(jnp.logical_and(for_last, d == 1))(lambda: give_back(n - 1, low, b))
            pl.when(from_low)(lambda: cols(low))
            pl.when(from_high)(lambda: cols(high))
            return carry

        lax.fori_loop(1, n, step, 0)
        for s in range(n):
            for b in range(2):
                @pl.when(taken(s, 0, n - 1))
                def _():
                    for copy in back_copies(j, s, b):
                        copy.wait_recv()

        for d in range(1, n):
            for e in range(1, n):
                at = begin.at[mod(j - d), mod(p - e)]
                rc(at, at, bzs.at[0], bpr.at[e, d], sibling).wait_recv()

    def reduce_copy(it, d):
        to = mod(r + d)
        return rc(part.at[it, to], rslots.at[it, d - 1], rs.at[it, d], rr.at[it, d], dev(a, to))

    def product(it):
        def block(to):
            at = pl.ds(pl.multiple_of(to * chunk, chunk), chunk)
            basis = bhi[...], blo[...]
            part[it, to] = dot3((ghi[at, :], glo[at, :]), basis, NN)

        for d in range(1, n):
            block(mod(r + d))
            reduce_copy(it, d).start()
        block(r)

    def spread_basis(source):
        def step(q, carry):
            at = pl.ds(pl.multiple_of(q * n * chunk, n * chunk), n * chunk)
            hi, lo = split(source(q).reshape(n * chunk, rank))
            bhi[at, :] = hi
            blo[at, :] = lo
            return carry

        lax.fori_loop(0, n, step, 0)

    def turned(it, turn):
        return lambda q: dot3(split(image[it, q].reshape(n * chunk, rank)), turn, NT)

    spread_basis(lambda q: begin[q])
    product(0)

    def line_copy(it, d, src_j, to_j):
        q, w = place(p, src_j)
        return rc(image.at[it, q, w], image.at[it, q, w], as_.at[it, d], ar.at[it, d], (i, to_j))

    def plane_copy(it, e, d):
        q, w = place(p, mod(j - d))
        return rc(image.at[it, q, w], image.at[it, q, w], ps.at[it, e, d], pr.at[it, e, d], (2 * peer(e) + c, j))

    def half_copy(it, e, d):
        q, w = place(source(e), mod(j - d))
        at = image.at[it, q, w, pl.ds((e - 1) * (chunk // 2), chunk // 2)]
        return rc(at, at, ps.at[it, 0 if e == 1 else 3, d], pr.at[it, 0 if e == 1 else 3, d], (2 * peer(3 - e) + c, j))

    def forward(it, d):
        if corner:
            for e in hops:
                q, w = place(source(e), mod(j - d))
                at = image.at[it, q, w]
                rc(at, at, ps.at[it, e, d], pr.at[it, e, d], sibling).wait_recv()
                half_copy(it, e, d).start()

    def arriving(it, e, d):
        q, w = place(source(e), mod(j - d))
        if not corner:
            return [(image.at[it, q, w], ps.at[it, e, d], pr.at[it, e, d])]
        return [
            (image.at[it, q, w, pl.ds(b * (chunk // 2), chunk // 2)], ps.at[it, 3 * b, d], pr.at[it, 3 * b, d])
            for b in range(2)
        ]

    def inner_one(it, e):
        to = mod(p + e)
        return rc(ipart.at[it, to], islots.at[it, e - 1], i1s.at[it, e], i1r.at[it, e], (2 * to + c, j))

    def inner_two(it, e):
        return rc(inner.at[it, p], inner.at[it, p], i2s.at[it, e], i2r.at[it, e], (2 * mod(p + e) + c, j))

    def iteration(it, carry):
        for d in range(1, n):
            reduce_copy(it, d).wait_recv()
        total = part[it, r]
        for d in range(1, n):
            total = total + rslots[it, d - 1]
        image[it, a, r] = total
        for d in range(1, n):
            line_copy(it, d, j, mod(j + d)).start()
        square = mul(total, total, TN)
        for d in range(1, n):
            line_copy(it, d, mod(j - d), j).wait_recv()
            q, w = place(p, mod(j - d))
            rows = image[it, q, w]
            square = square + mul(rows, rows, TN)
        ipart[it] = square.reshape(n, irows, rank)
        for e in range(1, n):
            inner_one(it, e).start()
        for e in range(1, n):
            inner_one(it, e).wait_recv()
        total = ipart[it, p]
        for e in range(1, n):
            total = total + islots[it, e - 1]
        inner[it, p] = total
        for e in range(1, n):
            inner_two(it, e).start()
        spread_needed = jnp.logical_or(odd, it < ITERS - 1)

        @pl.when(spread_needed)
        def _():
            for d in range(n):
                for e in hops:
                    plane_copy(it, e, d).start()

        for e in range(1, n):
            at = inner.at[it, mod(p - e)]
            rc(at, at, i2s.at[it, e], i2r.at[it, e], sibling).wait_recv()

        def between(step, steps):
            for d in range(n):
                if min(d, steps - 1) == step:
                    pl.when(spread_needed)(lambda: forward(it, d))

        inverse_factor(inner[it].reshape(rank, rank), work, linv, between)

        @pl.when(spread_needed)
        def _():
            for d in range(n):
                for e in far:
                    for at in arriving(it, e, d):
                        rc(at[0], at[0], at[1], at[2], sibling).wait_recv()


        @pl.when(it < ITERS - 1)
        def _():
            turn = split(linv[...])
            spread_basis(turned(it, turn))
            product(jnp.minimum(it + 1, ITERS - 1))

        for d in range(1, n):
            reduce_copy(it, d).wait_send()
            line_copy(it, d, j, mod(j + d)).wait_send()
        for e in range(1, n):
            inner_one(it, e).wait_send()
            inner_two(it, e).wait_send()

        @pl.when(spread_needed)
        def _():
            for d in range(n):
                for e in hops:
                    plane_copy(it, e, d).wait_send()
                    if corner:
                        half_copy(it, e, d).wait_send()

        return carry

    lax.fori_loop(0, ITERS, iteration, 0)

    last = ITERS - 1
    arows, bcols = out_ref.shape[1], out_ref.shape[2]
    give = rc(fxt, fxt, fs.at[0], fr.at[0], sibling)

    @pl.when(even)
    def _():
        turn = split(linv[...])
        rows = image[last, p].reshape(n * chunk, rank)
        fxt[...] = dot3(turn, split(rows), NT).astype(BF16)
        give.start()

    def part_copy(to):
        return rc(cpart.at[to], oslots.at[p], os_.at[to], or_.at[p], (to, j))

    middle = jnp.logical_and(j > 0, j < n - 1)
    work_here = jnp.logical_and(odd, middle)
    beside = jnp.logical_or(j == 1, j == n - 2)
    end = jnp.where(j <= 1, 0, n - 1)

    @pl.when(work_here)
    def _():
        mine = linv[pl.ds(pl.multiple_of(j * bcols, bcols), bcols), :]
        other = linv[pl.ds(pl.multiple_of(end * bcols, bcols), bcols), :]
        turn = split(jnp.concatenate([mine, other], axis=0))

        def step(q, carry):
            at = pl.ds(pl.multiple_of(q * n * chunk, n * chunk), n * chunk)
            fy[at, :] = turned(last, turn)(q).astype(BF16)
            return carry

        lax.fori_loop(0, n, step, 0)
        for q in range(2):
            for s in range(slabs):
                total = None
                for jj in range(n):
                    term = bdot(hw[2 * jj + q, s], fy[jj * hcols : (jj + 1) * hcols, :], NN)
                    total = term if total is None else total + term
                wsum[q, s] = total
        give.wait_recv()
        for s in range(slabs):
            total = None
            for q in range(2):
                tall = fxt[:, q * hrows : (q + 1) * hrows]
                hi, lo = split(wsum[q, s])
                term = bdot(tall, hi, NN) + bdot(tall, lo, NN)
                total = term if total is None else total + term
            for to in range(2 * n):
                cpart[to, s] = total[to * arows : (to + 1) * arows, :]
        for e in range(1, 2 * n):
            part_copy(lax.rem(i + e, 2 * n)).start()
        oslots[p] = cpart[i]

    pl.when(jnp.logical_and(odd, jnp.logical_not(middle)))(lambda: give.wait_recv())
    hand = rc(extra, final, es.at[0], er.at[0], (i, end))

    @pl.when(middle)
    def _():
        for pp in range(n):
            @pl.when(jnp.logical_or(even, p != pp))
            def _():
                rc(oslots.at[pp], oslots.at[pp], fs.at[0], or_.at[pp], sibling).wait_recv()

        total = oslots[0]
        for pp in range(1, n):
            total = total + oslots[pp]
        out_ref[...] = total[:, :, :bcols]
        extra[...] = total[:, :, bcols:]
        pl.when(beside)(lambda: hand.start())

    @pl.when(jnp.logical_not(middle))
    def _():
        hand.wait_recv()
        out_ref[...] = final[...]

    pl.when(even)(lambda: give.wait_send())
    pl.when(jnp.logical_and(middle, beside))(lambda: hand.wait_send())
    pl.when(even)(lambda: rc(h_ref, hw.at[ykey], ks.at[0], yr.at[ykey, 0], sibling).wait_send())
    pl.when(odd)(lambda: rc(h_ref, hw.at[i], ks.at[0], xr.at[i, 0], sibling).wait_send())
    pl.when(odd)(lambda: start_x(0).wait_send())
    for e in hops:
        plane_x(e).wait_send()
        start_x(e).wait_send()
    for b in range(2):
        pl.when(j < n - 1)(lambda: right(h_ref, ykey, b).wait_send())
        pl.when(j > 0)(lambda: left(h_ref, ykey, b).wait_send())

    if corner:
        @pl.when(even)
        def _():
            for e in hops:
                for q in range(2):
                    forward_x(e, q).wait_send()
                    forward_start(e, q).wait_send()

    @pl.when(work_here)
    def _():
        for e in range(1, 2 * n):
            part_copy(lax.rem(i + e, 2 * n)).wait_send()

    @pl.when(odd)
    def _():
        for d in range(1, n):
            rc(begin.at[j, p], begin.at[j, p], bzs.at[d], bzr.at[d], (i, mod(j + d))).wait_send()
            for e in range(1, n):
                at = begin.at[mod(j - d), p]
                rc(at, at, bps.at[e, d], bpr.at[e, d], (2 * mod(p + e) + 1, j)).wait_send()
        for s in range(n):
            for b in range(2):
                @pl.when(taken(s, 1, n - 2))
                def _():
                    for copy in back_copies(jnp.where(j == 1, 0, n - 1), s, b):
                        copy.wait_send()

        for d in range(1, n):
            for b in range(2):
                for q in range(2):
                    @pl.when(jnp.logical_and(j - d >= 0, j < n - 2))
                    def _():
                        s = jnp.maximum(j - d, 0) * 2 + q
                        right(hw.at[s], s, b).wait_send()

                    @pl.when(jnp.logical_and(j + d < n, j > 1))
                    def _():
                        s = jnp.minimum(j + d, n - 1) * 2 + q
                        left(hw.at[s], s, b).wait_send()


def on_device(history, start_x, start_y):
    nx, n = lax.axis_size("gx"), lax.axis_size("gy")
    slabs, hrows, hcols = history.shape
    rank = start_x.shape[1]
    rows = 2 * hrows
    assert nx == 2 * n and rows == hcols and n % 2 == 0 and n > 3 and slabs % 2 == 0
    chunk = rows // n
    dma = pltpu.SemaphoreType.DMA
    vmem = pltpu.VMEM
    arows, bcols = rank // nx, rank // n
    shape, pair = (slabs, arows, bcols), (slabs, arows, 2 * bcols)
    scratch = [
        vmem((2 * n, slabs, hrows, hcols), BF16),
        vmem((rows, n * rows), BF16), vmem((rows, n * rows), BF16),
        vmem((n, n, chunk, rank), F32),
        vmem((n * rows, rank), BF16), vmem((n * rows, rank), BF16),
        vmem((ITERS, n, chunk, rank), F32),
        vmem((ITERS, n - 1, chunk, rank), F32),
        vmem((ITERS, n, n, chunk, rank), F32),
        vmem((ITERS, n, rank // n, rank), F32),
        vmem((ITERS, n - 1, rank // n, rank), F32),
        vmem((ITERS, n, rank // n, rank), F32),
        vmem((rank, 2 * rank), F32),
        vmem((rank, rank), F32),
        vmem((rank, rows), BF16),
        vmem((n * rows, 2 * bcols), BF16),
        vmem((2, slabs, hrows, 2 * bcols), F32),
        vmem((nx,) + pair, F32),
        vmem((n,) + pair, F32),
        vmem((n, rows, hcols), BF16), vmem((n, rows, hcols), BF16),
        vmem(shape, F32), vmem(shape, F32),
        dma((1,)),
        dma((n,)), dma((nx, 2)),
        dma((n,)), dma((n,)),
        dma((n, n)), dma((n, n)),
        dma((n,)), dma((nx, 2)),
        dma((nx, 2)), dma((nx, 2)), dma((1,)), dma((nx, 2)),
        dma((ITERS, n)), dma((ITERS, n)),
        dma((ITERS, n)), dma((ITERS, n)),
        dma((ITERS, n, n)), dma((ITERS, n, n)),
        dma((ITERS, n)), dma((ITERS, n)),
        dma((ITERS, n)), dma((ITERS, n)),
        dma((1,)), dma((1,)),
        dma((nx,)), dma((n,)),
        dma((3, 2)), dma((3, 2)),
        dma((2, n, 2)), dma((2, n, 2)),
        dma((1,)), dma((1,)),
    ]
    return pl.pallas_call(
        functools.partial(kernel, n),
        out_shape=jax.ShapeDtypeStruct(shape, F32),
        in_specs=[pl.BlockSpec(memory_space=pltpu.VMEM)] * 3,
        out_specs=pl.BlockSpec(memory_space=pltpu.VMEM),
        scratch_shapes=scratch,
        compiler_params=pltpu.CompilerParams(
            collective_id=0, has_side_effects=True, vmem_limit_bytes=56 * 1024 * 1024
        ),
        name="tucker",
    )(history, start_x, start_y)


def solution(mesh):
    return jax.shard_map(
        on_device,
        mesh=mesh,
        in_specs=(P(None, "gx", "gy"), P("gx", None), P("gy", None)),
        out_specs=P(None, "gx", "gy"),
        check_vma=False,
    )
```

```python
import functools

import jax
import jax.numpy as jnp
from jax import lax
from jax.experimental import pallas as pl
from jax.experimental.pallas import tpu as pltpu
from jax.sharding import PartitionSpec as P

ITERS = 3
BLOCK = 64
HIGHEST = lax.Precision.HIGHEST
MESH = pl.DeviceIdType.MESH
F32, BF16 = jnp.float32, jnp.bfloat16
NN, NT, TN = ((1,), (0,)), ((1,), (1,)), ((0,), (0,))


def mul(a, b, dims):
    return lax.dot_general(a, b, (dims, ((), ())), precision=HIGHEST, preferred_element_type=F32)


def bdot(a, b, dims):
    return lax.dot_general(a, b, (dims, ((), ())), preferred_element_type=F32)


def split(v):
    hi = v.astype(BF16)
    return hi, (v - hi.astype(F32)).astype(BF16)


def dot3(a, b, dims):
    return bdot(a[0], b[0], dims) + (bdot(a[0], b[1], dims) + bdot(a[1], b[0], dims))


def eliminate(block):
    size = block.shape[0]
    sub = lax.broadcasted_iota(jnp.int32, (size, size), 0)
    lane = lax.broadcasted_iota(jnp.int32, (size, size), 1)
    eye = jnp.where(sub == lane, 1.0, 0.0).astype(F32)
    full = (8, 2 * size)
    sub8 = lax.broadcasted_iota(jnp.int32, full, 0)
    whole = jnp.concatenate([block, eye], axis=1)
    rows = [whole[t * 8 : t * 8 + 8] for t in range(size // 8)]
    for home in range(size // 8):
        k = home * 8
        tiles = range(home, size // 8)
        cols = {t: [jnp.broadcast_to(rows[t][:, k + m : k + m + 1], full) for m in range(8)] for t in tiles}
        piv = [[jnp.broadcast_to(cols[home][l][m : m + 1, :], full) for l in range(8)] for m in range(8)]
        held = [jnp.broadcast_to(rows[home][m : m + 1, :], full) for m in range(8)]
        inv = []
        for m in range(0, 8, 2):
            first, cross, second = piv[m][m], piv[m][m + 1], piv[m + 1][m + 1]
            inv0 = 1.0 / first
            inv1 = first * (1.0 / (first * second - cross * cross))
            ratio = cross * inv0
            inv += [inv0, inv1]
            held[m + 1] = held[m + 1] - ratio * held[m]
            for t in tiles:
                cols[t][m + 1] = cols[t][m + 1] - ratio * cols[t][m]
            for l in range(m + 2, 8):
                piv[m + 1][l] = piv[m + 1][l] - ratio * piv[m][l]
            for q in range(m + 2, 8):
                by0, by1 = piv[m][q] * inv0, piv[m + 1][q] * inv1
                for l in range(q, 8):
                    piv[q][l] = piv[q][l] - by0 * piv[m][l] - by1 * piv[m + 1][l]
                held[q] = held[q] - by0 * held[m] - by1 * held[m + 1]
                for t in tiles:
                    cols[t][q] = cols[t][q] - by0 * cols[t][m] - by1 * cols[t][m + 1]
        scaled = [held[m] * inv[m] for m in range(8)]
        for t in tiles:
            for m in range(8):
                col = cols[t][m]
                if t == home:
                    if m == 7:
                        continue
                    col = jnp.where(sub8 > m, col, 0.0)
                rows[t] = rows[t] - col * scaled[m]
    whole = jnp.concatenate(rows, axis=0)
    diag = jnp.sum(jnp.where(sub == lane, whole[:, :size], 0.0), axis=1, keepdims=True)
    return whole[:, size:] * (1.0 / jnp.sqrt(diag))


def inverse_factor(inner, work, out_ref, between):
    rank = inner.shape[0]
    sub = lax.broadcasted_iota(jnp.int32, (rank, rank), 0)
    lane = lax.broadcasted_iota(jnp.int32, (rank, rank), 1)
    same = sub == lane
    diag = jnp.where(same, inner, 0.0)
    tall = 1.0 / jnp.sqrt(jnp.sum(diag, axis=1, keepdims=True))
    wide = 1.0 / jnp.sqrt(jnp.sum(diag, axis=0, keepdims=True))
    work[:, :rank] = inner * tall * wide
    work[:, rank:] = jnp.where(same, 1.0, 0.0).astype(F32)
    for step, at in enumerate(range(0, rank, BLOCK)):
        inverse = eliminate(work[at : at + BLOCK, at : at + BLOCK])
        top = mul(inverse, work[at : at + BLOCK, :], NN)
        out_ref[at : at + BLOCK, :] = top[:, rank:] * wide
        if at + BLOCK < rank:
            left = top[:, at + BLOCK : rank]
            work[at + BLOCK :, :] = work[at + BLOCK :, :] - mul(left, top, TN)
        between(step, rank // BLOCK)


def kernel(
    n, h_ref, bx_ref, by_ref, out_ref,
    hw, ghi, glo, begin, bhi, blo, part, rslots, image, ipart, islots, inner, work, linv, fxt, fy, wsum, cpart, oslots, back_hi, back_lo, extra, final,
    own, bs, br, bzs, bzr, bps, bpr, xs, xr, zr, zl, ks, yr, rs, rr, as_, ar, ps, pr, i1s, i1r, i2s, i2r, fs, fr, os_, or_, fxs, fbs, gs, gr, es, er,
):
    i, j = lax.axis_index("gx"), lax.axis_index("gy")
    p, c = i // 2, lax.rem(i, 2)
    even = c == 0
    odd = c == 1
    slabs, hrows, hcols = h_ref.shape
    rank = bx_ref.shape[1]
    chunk = image.shape[3]
    irows = rank // n
    sibling = (i + 1 - 2 * c, j)

    def mod(v):
        return lax.rem(v + n, n)

    def rc(src, dst, ss, rsem, dev):
        return pltpu.make_async_remote_copy(
            src_ref=src, dst_ref=dst, send_sem=ss, recv_sem=rsem, device_id=dev, device_id_type=MESH
        )

    a = jnp.where(even, p, j)
    r = jnp.where(even, j, p)

    def dev(aa, rr_):
        return (jnp.where(even, 2 * aa, 2 * rr_ + 1), jnp.where(even, rr_, aa))

    def place(pp, jj):
        return jnp.where(even, pp, jj), jnp.where(even, jj, pp)

    corner = n == 4
    hops = (1, 2) if corner else tuple(range(1, n))
    far = (3,) if corner else hops

    def across(e):
        return (p + 1 - 2 * lax.rem(p, 2), lax.rem(p + 2, n), n - 1 - p)[e - 1]

    def peer(e):
        return across(e) if corner else mod(p + e)

    def source(e):
        return across(e) if corner else mod(p - e)

    barrier = pltpu.get_barrier_semaphore()
    for e in range(1, 2 * n):
        pl.semaphore_signal(barrier, inc=1, device_id=(lax.rem(i + e, 2 * n), j), device_id_type=MESH)
    for d in range(1, n):
        for cc in range(2):
            pl.semaphore_signal(barrier, inc=1, device_id=(2 * p + cc, mod(j + d)), device_id_type=MESH)
    pl.semaphore_wait(barrier, 2 * n - 1 + 2 * (n - 1))

    @pl.when(even)
    def _():
        for q in range(n // 2):
            begin[p, q] = bx_ref[q * chunk : (q + 1) * chunk, :]

    @pl.when(odd)
    def _():
        for q in range(n):
            begin[j, q] = by_ref[q * chunk : (q + 1) * chunk, :]
        for d in range(1, n):
            rc(begin.at[j, p], begin.at[j, p], bzs.at[d], bzr.at[d], (i, mod(j + d))).start()

    ykey = j * 2 + c

    width = hcols // 2
    pieces = [pl.ds(b * width, width) for b in range(2)]

    def right(src, s, b):
        to = (2 * p + 1, jnp.minimum(j + 1, n - 1))
        return rc(src.at[:, :, pieces[b]], hw.at[s, :, :, pieces[b]], zr.at[s, b], yr.at[s, b], to)

    def left(src, s, b):
        to = (2 * p + 1, jnp.maximum(j - 1, 0))
        return rc(src.at[:, :, pieces[b]], hw.at[s, :, :, pieces[b]], zl.at[s, b], yr.at[s, b], to)

    for b in range(2):
        pl.when(j < n - 1)(lambda: right(h_ref, ykey, b).start())
        pl.when(j > 0)(lambda: left(h_ref, ykey, b).start())

    def own_copy():
        return pltpu.make_async_copy(h_ref, hw.at[jnp.where(even, i, ykey)], own.at[0])

    own_copy().start()
    pl.when(even)(lambda: rc(h_ref, hw.at[ykey], ks.at[0], yr.at[ykey, 0], sibling).start())
    pl.when(odd)(lambda: rc(h_ref, hw.at[i], ks.at[0], xr.at[i, 0], sibling).start())

    half = n // 2

    bxc = bx_ref.reshape(half, chunk, rank)

    def start_x(e):
        dst = begin.at[p, pl.ds(c * half, half)]
        return rc(bxc, dst, bs.at[e], br.at[i, 0], (2 * (p if e == 0 else peer(e)), j))

    def plane_x(e):
        return rc(h_ref, hw.at[i], xs.at[e], xr.at[i, 0], (2 * peer(e), j))

    sh = slabs // 2

    def forward_x(e, q):
        slot = 2 * source(e) + q
        at = hw.at[slot, pl.ds((e - 1) * sh, sh)]
        return rc(at, at, fxs.at[e, q], xr.at[slot, e - 1], (2 * peer(3 - e), j))

    def forward_start(e, q):
        at = begin.at[source(e), q * half + e - 1]
        return rc(at, at, fbs.at[e, q], br.at[2 * source(e) + q, e - 1], (2 * peer(3 - e), j))

    pl.when(odd)(lambda: start_x(0).start())
    for e in hops:
        plane_x(e).start()
    for e in hops:
        start_x(e).start()
    own_copy().wait()

    @pl.when(even)
    def _():
        rc(h_ref, hw.at[i + 1], ks.at[0], xr.at[i + 1, 0], sibling).wait_recv()

        def cols(slot):
            for q in range(2):
                total = None
                for s in range(slabs):
                    term = bdot(hw[2 * p + q, s], hw[slot, s], NT)
                    total = term if total is None else total + term
                hi, lo = split(total)
                at = pl.ds(pl.multiple_of(slot * hrows, hrows), hrows)
                ghi[q * hrows : (q + 1) * hrows, at] = hi
                glo[q * hrows : (q + 1) * hrows, at] = lo

        def all_cols(slots):
            def step(t, carry):
                slot = slots[0]
                for u in range(1, len(slots)):
                    slot = jnp.where(t == u, slots[u], slot)
                cols(slot)
                return carry

            lax.fori_loop(0, len(slots), step, 0)

        for e in hops:
            for q in range(2):
                slot = 2 * source(e) + q
                rc(h_ref, hw.at[slot], ks.at[0], xr.at[slot, 0], sibling).wait_recv()
                if corner:
                    forward_x(e, q).start()
        all_cols([2 * p, 2 * p + 1] + [2 * source(e) + q for e in hops for q in range(2)])
        rc(bxc, begin.at[p, pl.ds(half, half)], ks.at[0], br.at[i + 1, 0], sibling).wait_recv()
        for e in hops:
            for q in range(2):
                pp = source(e)
                rc(bxc, begin.at[pp, pl.ds(q * half, half)], ks.at[0], br.at[2 * pp + q, 0], sibling).wait_recv()
                if corner:
                    forward_start(e, q).start()
        if corner:
            for q in range(2):
                slot = 2 * source(3) + q
                for b in range(2):
                    at = hw.at[slot, pl.ds(b * sh, sh)]
                    rc(at, at, ks.at[0], xr.at[slot, b], sibling).wait_recv()
            all_cols([2 * source(3), 2 * source(3) + 1])
            for q in range(2):
                for b in range(2):
                    at = begin.at[source(3), q * half + b]
                    rc(at, at, ks.at[0], br.at[2 * source(3) + q, b], sibling).wait_recv()

    def taken(s, first, last):
        return jnp.logical_or(jnp.logical_and(j == first, s > 1), jnp.logical_and(j == last, s < n - 2))

    def back_copies(to, s, b):
        at = pl.ds(pl.multiple_of(s * hcols + b * width, width), width)
        return [
            rc(src.at[s, :, pieces[b]], dst.at[:, at], gs.at[m, s, b], gr.at[m, s, b], (i, to))
            for m, (src, dst) in enumerate(((back_hi, ghi), (back_lo, glo)))
        ]

    @pl.when(odd)
    def _():
        for d in range(1, n):
            jj = mod(j - d)
            rc(begin.at[jj, p], begin.at[jj, p], bzs.at[0], bzr.at[d], sibling).wait_recv()
            for e in range(1, n):
                rc(begin.at[jj, p], begin.at[jj, p], bps.at[e, d], bpr.at[e, d], (2 * mod(p + e) + 1, j)).start()
        rc(h_ref, hw.at[j * 2], ks.at[0], yr.at[j * 2, 0], sibling).wait_recv()

        def cols(jj):
            total = None
            for q in range(2):
                for s in range(slabs):
                    term = bdot(hw[2 * j + q, s], hw[2 * jj + q, s], TN)
                    total = term if total is None else total + term
            hi, lo = split(total)
            at = pl.ds(pl.multiple_of(jj * hcols, hcols), hcols)
            ghi[:, at] = hi
            glo[:, at] = lo

        cols(j)

        def give_back(base, s, b):
            total = None
            for q in range(2):
                for t in range(slabs):
                    term = bdot(hw[2 * base + q, t], hw[2 * s + q, t, :, pieces[b]], TN)
                    total = term if total is None else total + term
            back_hi[s, :, pieces[b]], back_lo[s, :, pieces[b]] = split(total)
            for copy in back_copies(base, s, b):
                copy.start()

        def step(d, carry):
            low, high = jnp.maximum(j - d, 0), jnp.minimum(j + d, n - 1)
            from_low = jnp.logical_and(j - d >= 0, jnp.logical_or(d == 1, j < n - 1))
            from_high = jnp.logical_and(j + d < n, jnp.logical_or(d == 1, j > 0))
            for_first = jnp.logical_and(from_high, j == 1)
            for_last = jnp.logical_and(from_low, j == n - 2)
            for b in range(2):
                for q in range(2):
                    @pl.when(from_low)
                    def _():
                        s = low * 2 + q
                        right(hw.at[s], s, b).wait_recv()
                        pl.when(j < n - 2)(lambda: right(hw.at[s], s, b).start())

                    @pl.when(from_high)
                    def _():
                        s = high * 2 + q
                        left(hw.at[s], s, b).wait_recv()
                        pl.when(j > 1)(lambda: left(hw.at[s], s, b).start())

                pl.when(jnp.logical_and(for_first, d > 1))(lambda: give_back(0, high, b))
                pl.when(jnp.logical_and(for_last, d > 1))(lambda: give_back(n - 1, low, b))
            for b in range(2):
                pl.when(jnp.logical_and(for_first, d == 1))(lambda: give_back(0, high, b))
                pl.when(jnp.logical_and(for_last, d == 1))(lambda: give_back(n - 1, low, b))
            pl.when(from_low)(lambda: cols(low))
            pl.when(from_high)(lambda: cols(high))
            return carry

        lax.fori_loop(1, n, step, 0)
        for s in range(n):
            for b in range(2):
                @pl.when(taken(s, 0, n - 1))
                def _():
                    for copy in back_copies(j, s, b):
                        copy.wait_recv()

        for d in range(1, n):
            for e in range(1, n):
                at = begin.at[mod(j - d), mod(p - e)]
                rc(at, at, bzs.at[0], bpr.at[e, d], sibling).wait_recv()

    def reduce_copy(it, d):
        to = mod(r + d)
        return rc(part.at[it, to], rslots.at[it, d - 1], rs.at[it, d], rr.at[it, d], dev(a, to))

    def product(it):
        def block(to):
            at = pl.ds(pl.multiple_of(to * chunk, chunk), chunk)
            basis = bhi[...], blo[...]
            part[it, to] = dot3((ghi[at, :], glo[at, :]), basis, NN)

        for d in range(1, n):
            block(mod(r + d))
            reduce_copy(it, d).start()
        block(r)

    def spread_basis(source):
        def step(q, carry):
            at = pl.ds(pl.multiple_of(q * n * chunk, n * chunk), n * chunk)
            hi, lo = split(source(q).reshape(n * chunk, rank))
            bhi[at, :] = hi
            blo[at, :] = lo
            return carry

        lax.fori_loop(0, n, step, 0)

    def turned(it, turn):
        return lambda q: dot3(split(image[it, q].reshape(n * chunk, rank)), turn, NT)

    spread_basis(lambda q: begin[q])
    product(0)

    def line_copy(it, d, src_j, to_j):
        q, w = place(p, src_j)
        return rc(image.at[it, q, w], image.at[it, q, w], as_.at[it, d], ar.at[it, d], (i, to_j))

    def plane_copy(it, e, d):
        q, w = place(p, mod(j - d))
        return rc(image.at[it, q, w], image.at[it, q, w], ps.at[it, e, d], pr.at[it, e, d], (2 * peer(e) + c, j))

    def half_copy(it, e, d):
        q, w = place(source(e), mod(j - d))
        at = image.at[it, q, w, pl.ds((e - 1) * (chunk // 2), chunk // 2)]
        return rc(at, at, ps.at[it, 0 if e == 1 else 3, d], pr.at[it, 0 if e == 1 else 3, d], (2 * peer(3 - e) + c, j))

    def forward(it, d):
        if corner:
            for e in hops:
                q, w = place(source(e), mod(j - d))
                at = image.at[it, q, w]
                rc(at, at, ps.at[it, e, d], pr.at[it, e, d], sibling).wait_recv()
                half_copy(it, e, d).start()

    def arriving(it, e, d):
        q, w = place(source(e), mod(j - d))
        if not corner:
            return [(image.at[it, q, w], ps.at[it, e, d], pr.at[it, e, d])]
        return [
            (image.at[it, q, w, pl.ds(b * (chunk // 2), chunk // 2)], ps.at[it, 3 * b, d], pr.at[it, 3 * b, d])
            for b in range(2)
        ]

    def inner_one(it, e):
        to = mod(p + e)
        return rc(ipart.at[it, to], islots.at[it, e - 1], i1s.at[it, e], i1r.at[it, e], (2 * to + c, j))

    def inner_two(it, e):
        return rc(inner.at[it, p], inner.at[it, p], i2s.at[it, e], i2r.at[it, e], (2 * mod(p + e) + c, j))

    def iteration(it, carry):
        for d in range(1, n):
            reduce_copy(it, d).wait_recv()
        total = part[it, r]
        for d in range(1, n):
            total = total + rslots[it, d - 1]
        image[it, a, r] = total
        for d in range(1, n):
            line_copy(it, d, j, mod(j + d)).start()
        spread_needed = jnp.logical_or(odd, it < ITERS - 1)

        @pl.when(spread_needed)
        def _():
            for e in hops:
                plane_copy(it, e, 0).start()

        square = mul(total, total, TN)
        for d in range(1, n):
            line_copy(it, d, mod(j - d), j).wait_recv()
            q, w = place(p, mod(j - d))
            rows = image[it, q, w]
            square = square + mul(rows, rows, TN)
        ipart[it] = square.reshape(n, irows, rank)
        for e in range(1, n):
            inner_one(it, e).start()
        pl.when(spread_needed)(lambda: forward(it, 0))
        for e in range(1, n):
            inner_one(it, e).wait_recv()
        total = ipart[it, p]
        for e in range(1, n):
            total = total + islots[it, e - 1]
        inner[it, p] = total
        for e in range(1, n):
            inner_two(it, e).start()

        @pl.when(spread_needed)
        def _():
            for d in range(1, n):
                for e in hops:
                    plane_copy(it, e, d).start()

        for e in range(1, n):
            at = inner.at[it, mod(p - e)]
            rc(at, at, i2s.at[it, e], i2r.at[it, e], sibling).wait_recv()

        def between(step, steps):
            for d in range(1, n):
                if min(d - 1, steps - 1) == step:
                    pl.when(spread_needed)(lambda: forward(it, d))

        inverse_factor(inner[it].reshape(rank, rank), work, linv, between)

        @pl.when(spread_needed)
        def _():
            for d in range(n):
                for e in far:
                    for at in arriving(it, e, d):
                        rc(at[0], at[0], at[1], at[2], sibling).wait_recv()


        @pl.when(it < ITERS - 1)
        def _():
            turn = split(linv[...])
            spread_basis(turned(it, turn))
            product(jnp.minimum(it + 1, ITERS - 1))

        for d in range(1, n):
            reduce_copy(it, d).wait_send()
            line_copy(it, d, j, mod(j + d)).wait_send()
        for e in range(1, n):
            inner_one(it, e).wait_send()
            inner_two(it, e).wait_send()

        @pl.when(spread_needed)
        def _():
            for d in range(n):
                for e in hops:
                    plane_copy(it, e, d).wait_send()
                    if corner:
                        half_copy(it, e, d).wait_send()

        return carry

    lax.fori_loop(0, ITERS, iteration, 0)

    last = ITERS - 1
    arows, bcols = out_ref.shape[1], out_ref.shape[2]
    give = rc(fxt, fxt, fs.at[0], fr.at[0], sibling)

    @pl.when(even)
    def _():
        turn = split(linv[...])
        rows = image[last, p].reshape(n * chunk, rank)
        fxt[...] = dot3(turn, split(rows), NT).astype(BF16)
        give.start()

    def part_copy(to):
        return rc(cpart.at[to], oslots.at[p], os_.at[to], or_.at[p], (to, j))

    middle = jnp.logical_and(j > 0, j < n - 1)
    work_here = jnp.logical_and(odd, middle)
    beside = jnp.logical_or(j == 1, j == n - 2)
    end = jnp.where(j <= 1, 0, n - 1)

    @pl.when(work_here)
    def _():
        mine = linv[pl.ds(pl.multiple_of(j * bcols, bcols), bcols), :]
        other = linv[pl.ds(pl.multiple_of(end * bcols, bcols), bcols), :]
        turn = split(jnp.concatenate([mine, other], axis=0))

        def step(q, carry):
            at = pl.ds(pl.multiple_of(q * n * chunk, n * chunk), n * chunk)
            fy[at, :] = turned(last, turn)(q).astype(BF16)
            return carry

        lax.fori_loop(0, n, step, 0)
        for q in range(2):
            for s in range(slabs):
                total = None
                for jj in range(n):
                    term = bdot(hw[2 * jj + q, s], fy[jj * hcols : (jj + 1) * hcols, :], NN)
                    total = term if total is None else total + term
                wsum[q, s] = total
        give.wait_recv()
        for s in range(slabs):
            total = None
            for q in range(2):
                tall = fxt[:, q * hrows : (q + 1) * hrows]
                hi, lo = split(wsum[q, s])
                term = bdot(tall, hi, NN) + bdot(tall, lo, NN)
                total = term if total is None else total + term
            for to in range(2 * n):
                cpart[to, s] = total[to * arows : (to + 1) * arows, :]
        for e in range(1, 2 * n):
            part_copy(lax.rem(i + e, 2 * n)).start()
        oslots[p] = cpart[i]

    pl.when(jnp.logical_and(odd, jnp.logical_not(middle)))(lambda: give.wait_recv())
    hand = rc(extra, final, es.at[0], er.at[0], (i, end))

    @pl.when(middle)
    def _():
        for pp in range(n):
            @pl.when(jnp.logical_or(even, p != pp))
            def _():
                rc(oslots.at[pp], oslots.at[pp], fs.at[0], or_.at[pp], sibling).wait_recv()

        total = oslots[0]
        for pp in range(1, n):
            total = total + oslots[pp]
        out_ref[...] = total[:, :, :bcols]
        extra[...] = total[:, :, bcols:]
        pl.when(beside)(lambda: hand.start())

    @pl.when(jnp.logical_not(middle))
    def _():
        hand.wait_recv()
        out_ref[...] = final[...]

    pl.when(even)(lambda: give.wait_send())
    pl.when(jnp.logical_and(middle, beside))(lambda: hand.wait_send())
    pl.when(even)(lambda: rc(h_ref, hw.at[ykey], ks.at[0], yr.at[ykey, 0], sibling).wait_send())
    pl.when(odd)(lambda: rc(h_ref, hw.at[i], ks.at[0], xr.at[i, 0], sibling).wait_send())
    pl.when(odd)(lambda: start_x(0).wait_send())
    for e in hops:
        plane_x(e).wait_send()
        start_x(e).wait_send()
    for b in range(2):
        pl.when(j < n - 1)(lambda: right(h_ref, ykey, b).wait_send())
        pl.when(j > 0)(lambda: left(h_ref, ykey, b).wait_send())

    if corner:
        @pl.when(even)
        def _():
            for e in hops:
                for q in range(2):
                    forward_x(e, q).wait_send()
                    forward_start(e, q).wait_send()

    @pl.when(work_here)
    def _():
        for e in range(1, 2 * n):
            part_copy(lax.rem(i + e, 2 * n)).wait_send()

    @pl.when(odd)
    def _():
        for d in range(1, n):
            rc(begin.at[j, p], begin.at[j, p], bzs.at[d], bzr.at[d], (i, mod(j + d))).wait_send()
            for e in range(1, n):
                at = begin.at[mod(j - d), p]
                rc(at, at, bps.at[e, d], bpr.at[e, d], (2 * mod(p + e) + 1, j)).wait_send()
        for s in range(n):
            for b in range(2):
                @pl.when(taken(s, 1, n - 2))
                def _():
                    for copy in back_copies(jnp.where(j == 1, 0, n - 1), s, b):
                        copy.wait_send()

        for d in range(1, n):
            for b in range(2):
                for q in range(2):
                    @pl.when(jnp.logical_and(j - d >= 0, j < n - 2))
                    def _():
                        s = jnp.maximum(j - d, 0) * 2 + q
                        right(hw.at[s], s, b).wait_send()

                    @pl.when(jnp.logical_and(j + d < n, j > 1))
                    def _():
                        s = jnp.minimum(j + d, n - 1) * 2 + q
                        left(hw.at[s], s, b).wait_send()


def on_device(history, start_x, start_y):
    nx, n = lax.axis_size("gx"), lax.axis_size("gy")
    slabs, hrows, hcols = history.shape
    rank = start_x.shape[1]
    rows = 2 * hrows
    assert nx == 2 * n and rows == hcols and n % 2 == 0 and n > 3 and slabs % 2 == 0
    chunk = rows // n
    dma = pltpu.SemaphoreType.DMA
    vmem = pltpu.VMEM
    arows, bcols = rank // nx, rank // n
    shape, pair = (slabs, arows, bcols), (slabs, arows, 2 * bcols)
    scratch = [
        vmem((2 * n, slabs, hrows, hcols), BF16),
        vmem((rows, n * rows), BF16), vmem((rows, n * rows), BF16),
        vmem((n, n, chunk, rank), F32),
        vmem((n * rows, rank), BF16), vmem((n * rows, rank), BF16),
        vmem((ITERS, n, chunk, rank), F32),
        vmem((ITERS, n - 1, chunk, rank), F32),
        vmem((ITERS, n, n, chunk, rank), F32),
        vmem((ITERS, n, rank // n, rank), F32),
        vmem((ITERS, n - 1, rank // n, rank), F32),
        vmem((ITERS, n, rank // n, rank), F32),
        vmem((rank, 2 * rank), F32),
        vmem((rank, rank), F32),
        vmem((rank, rows), BF16),
        vmem((n * rows, 2 * bcols), BF16),
        vmem((2, slabs, hrows, 2 * bcols), F32),
        vmem((nx,) + pair, F32),
        vmem((n,) + pair, F32),
        vmem((n, rows, hcols), BF16), vmem((n, rows, hcols), BF16),
        vmem(shape, F32), vmem(shape, F32),
        dma((1,)),
        dma((n,)), dma((nx, 2)),
        dma((n,)), dma((n,)),
        dma((n, n)), dma((n, n)),
        dma((n,)), dma((nx, 2)),
        dma((nx, 2)), dma((nx, 2)), dma((1,)), dma((nx, 2)),
        dma((ITERS, n)), dma((ITERS, n)),
        dma((ITERS, n)), dma((ITERS, n)),
        dma((ITERS, n, n)), dma((ITERS, n, n)),
        dma((ITERS, n)), dma((ITERS, n)),
        dma((ITERS, n)), dma((ITERS, n)),
        dma((1,)), dma((1,)),
        dma((nx,)), dma((n,)),
        dma((3, 2)), dma((3, 2)),
        dma((2, n, 2)), dma((2, n, 2)),
        dma((1,)), dma((1,)),
    ]
    return pl.pallas_call(
        functools.partial(kernel, n),
        out_shape=jax.ShapeDtypeStruct(shape, F32),
        in_specs=[pl.BlockSpec(memory_space=pl.ANY)] + [pl.BlockSpec(memory_space=pltpu.VMEM)] * 2,
        out_specs=pl.BlockSpec(memory_space=pltpu.VMEM),
        scratch_shapes=scratch,
        compiler_params=pltpu.CompilerParams(
            collective_id=0, has_side_effects=True, vmem_limit_bytes=56 * 1024 * 1024
        ),
        name="tucker",
    )(history, start_x, start_y)


def solution(mesh):
    return jax.shard_map(
        on_device,
        mesh=mesh,
        in_specs=(P(None, "gx", "gy"), P("gx", None), P("gy", None)),
        out_specs=P(None, "gx", "gy"),
        check_vma=False,
    )
```

```python
import functools

import jax
import jax.numpy as jnp
from jax import lax
from jax.experimental import pallas as pl
from jax.experimental.pallas import tpu as pltpu
from jax.sharding import PartitionSpec as P

ITERS = 3
BLOCK = 64
HIGHEST = lax.Precision.HIGHEST
MESH = pl.DeviceIdType.MESH
F32, BF16 = jnp.float32, jnp.bfloat16
NN, NT, TN = ((1,), (0,)), ((1,), (1,)), ((0,), (0,))


def mul(a, b, dims):
    return lax.dot_general(a, b, (dims, ((), ())), precision=HIGHEST, preferred_element_type=F32)


def bdot(a, b, dims):
    return lax.dot_general(a, b, (dims, ((), ())), preferred_element_type=F32)


def split(v):
    hi = v.astype(BF16)
    return hi, (v - hi.astype(F32)).astype(BF16)


def dot3(a, b, dims):
    return bdot(a[0], b[0], dims) + (bdot(a[0], b[1], dims) + bdot(a[1], b[0], dims))


def eliminate(block):
    size = block.shape[0]
    sub = lax.broadcasted_iota(jnp.int32, (size, size), 0)
    lane = lax.broadcasted_iota(jnp.int32, (size, size), 1)
    eye = jnp.where(sub == lane, 1.0, 0.0).astype(F32)
    full = (8, 2 * size)
    sub8 = lax.broadcasted_iota(jnp.int32, full, 0)
    whole = jnp.concatenate([block, eye], axis=1)
    rows = [whole[t * 8 : t * 8 + 8] for t in range(size // 8)]
    for home in range(size // 8):
        k = home * 8
        tiles = range(home, size // 8)
        cols = {t: [jnp.broadcast_to(rows[t][:, k + m : k + m + 1], full) for m in range(8)] for t in tiles}
        piv = [[jnp.broadcast_to(cols[home][l][m : m + 1, :], full) for l in range(8)] for m in range(8)]
        held = [jnp.broadcast_to(rows[home][m : m + 1, :], full) for m in range(8)]
        inv = []
        for m in range(0, 8, 2):
            first, cross, second = piv[m][m], piv[m][m + 1], piv[m + 1][m + 1]
            inv0 = 1.0 / first
            inv1 = first * (1.0 / (first * second - cross * cross))
            ratio = cross * inv0
            inv += [inv0, inv1]
            held[m + 1] = held[m + 1] - ratio * held[m]
            for t in tiles:
                cols[t][m + 1] = cols[t][m + 1] - ratio * cols[t][m]
            for l in range(m + 2, 8):
                piv[m + 1][l] = piv[m + 1][l] - ratio * piv[m][l]
            for q in range(m + 2, 8):
                by0, by1 = piv[m][q] * inv0, piv[m + 1][q] * inv1
                for l in range(q, 8):
                    piv[q][l] = piv[q][l] - by0 * piv[m][l] - by1 * piv[m + 1][l]
                held[q] = held[q] - by0 * held[m] - by1 * held[m + 1]
                for t in tiles:
                    cols[t][q] = cols[t][q] - by0 * cols[t][m] - by1 * cols[t][m + 1]
        scaled = [held[m] * inv[m] for m in range(8)]
        for t in tiles:
            for m in range(8):
                col = cols[t][m]
                if t == home:
                    if m == 7:
                        continue
                    col = jnp.where(sub8 > m, col, 0.0)
                rows[t] = rows[t] - col * scaled[m]
    whole = jnp.concatenate(rows, axis=0)
    diag = jnp.sum(jnp.where(sub == lane, whole[:, :size], 0.0), axis=1, keepdims=True)
    return whole[:, size:] * (1.0 / jnp.sqrt(diag))


def inverse_factor(inner, work, out_ref, between):
    rank = inner.shape[0]
    sub = lax.broadcasted_iota(jnp.int32, (rank, rank), 0)
    lane = lax.broadcasted_iota(jnp.int32, (rank, rank), 1)
    same = sub == lane
    diag = jnp.where(same, inner, 0.0)
    tall = 1.0 / jnp.sqrt(jnp.sum(diag, axis=1, keepdims=True))
    wide = 1.0 / jnp.sqrt(jnp.sum(diag, axis=0, keepdims=True))
    work[:, :rank] = inner * tall * wide
    work[:, rank:] = jnp.where(same, 1.0, 0.0).astype(F32)
    for step, at in enumerate(range(0, rank, BLOCK)):
        inverse = eliminate(work[at : at + BLOCK, at : at + BLOCK])
        top = mul(inverse, work[at : at + BLOCK, :], NN)
        out_ref[at : at + BLOCK, :] = top[:, rank:] * wide
        if at + BLOCK < rank:
            left = top[:, at + BLOCK : rank]
            work[at + BLOCK :, :] = work[at + BLOCK :, :] - mul(left, top, TN)
        between(step, rank // BLOCK)


def kernel(
    n, h_ref, bx_ref, by_ref, out_ref,
    hw, ghi, glo, begin, bhi, blo, part, rslots, image, ipart, islots, inner, work, linv, fxt, fy, wsum, cpart, oslots, back_hi, back_lo, extra, final,
    own, bs, br, bzs, bzr, bps, bpr, xs, xr, zr, zl, ks, yr, rs, rr, as_, ar, ps, pr, i1s, i1r, i2s, i2r, fs, fr, os_, or_, fxs, fbs, gs, gr, es, er,
):
    i, j = lax.axis_index("gx"), lax.axis_index("gy")
    p, c = i // 2, lax.rem(i, 2)
    even = c == 0
    odd = c == 1
    slabs, hrows, hcols = h_ref.shape
    rank = bx_ref.shape[1]
    chunk = image.shape[3]
    side = rank // 2
    irows = 3 * side // n
    sibling = (i + 1 - 2 * c, j)

    def mod(v):
        return lax.rem(v + n, n)

    def rc(src, dst, ss, rsem, dev):
        return pltpu.make_async_remote_copy(
            src_ref=src, dst_ref=dst, send_sem=ss, recv_sem=rsem, device_id=dev, device_id_type=MESH
        )

    a = jnp.where(even, p, j)
    r = jnp.where(even, j, p)

    def dev(aa, rr_):
        return (jnp.where(even, 2 * aa, 2 * rr_ + 1), jnp.where(even, rr_, aa))

    def place(pp, jj):
        return jnp.where(even, pp, jj), jnp.where(even, jj, pp)

    corner = n == 4
    hops = (1, 2) if corner else tuple(range(1, n))
    far = (3,) if corner else hops

    def across(e):
        return (p + 1 - 2 * lax.rem(p, 2), lax.rem(p + 2, n), n - 1 - p)[e - 1]

    def peer(e):
        return across(e) if corner else mod(p + e)

    def source(e):
        return across(e) if corner else mod(p - e)

    barrier = pltpu.get_barrier_semaphore()
    for e in range(1, 2 * n):
        pl.semaphore_signal(barrier, inc=1, device_id=(lax.rem(i + e, 2 * n), j), device_id_type=MESH)
    for d in range(1, n):
        for cc in range(2):
            pl.semaphore_signal(barrier, inc=1, device_id=(2 * p + cc, mod(j + d)), device_id_type=MESH)
    pl.semaphore_wait(barrier, 2 * n - 1 + 2 * (n - 1))

    @pl.when(even)
    def _():
        for q in range(n // 2):
            begin[p, q] = bx_ref[q * chunk : (q + 1) * chunk, :]

    @pl.when(odd)
    def _():
        for q in range(n):
            begin[j, q] = by_ref[q * chunk : (q + 1) * chunk, :]
        for d in range(1, n):
            rc(begin.at[j, p], begin.at[j, p], bzs.at[d], bzr.at[d], (i, mod(j + d))).start()

    ykey = j * 2 + c

    width = hcols // 2
    pieces = [pl.ds(b * width, width) for b in range(2)]

    def right(src, s, b):
        to = (2 * p + 1, jnp.minimum(j + 1, n - 1))
        return rc(src.at[:, :, pieces[b]], hw.at[s, :, :, pieces[b]], zr.at[s, b], yr.at[s, b], to)

    def left(src, s, b):
        to = (2 * p + 1, jnp.maximum(j - 1, 0))
        return rc(src.at[:, :, pieces[b]], hw.at[s, :, :, pieces[b]], zl.at[s, b], yr.at[s, b], to)

    for b in range(2):
        pl.when(j < n - 1)(lambda: right(h_ref, ykey, b).start())
        pl.when(j > 0)(lambda: left(h_ref, ykey, b).start())

    def own_copy():
        return pltpu.make_async_copy(h_ref, hw.at[jnp.where(even, i, ykey)], own.at[0])

    own_copy().start()
    pl.when(even)(lambda: rc(h_ref, hw.at[ykey], ks.at[0], yr.at[ykey, 0], sibling).start())
    pl.when(odd)(lambda: rc(h_ref, hw.at[i], ks.at[0], xr.at[i, 0], sibling).start())

    half = n // 2

    bxc = bx_ref.reshape(half, chunk, rank)

    def start_x(e):
        dst = begin.at[p, pl.ds(c * half, half)]
        return rc(bxc, dst, bs.at[e], br.at[i, 0], (2 * (p if e == 0 else peer(e)), j))

    def plane_x(e):
        return rc(h_ref, hw.at[i], xs.at[e], xr.at[i, 0], (2 * peer(e), j))

    sh = slabs // 2

    def forward_x(e, q):
        slot = 2 * source(e) + q
        at = hw.at[slot, pl.ds((e - 1) * sh, sh)]
        return rc(at, at, fxs.at[e, q], xr.at[slot, e - 1], (2 * peer(3 - e), j))

    def forward_start(e, q):
        at = begin.at[source(e), q * half + e - 1]
        return rc(at, at, fbs.at[e, q], br.at[2 * source(e) + q, e - 1], (2 * peer(3 - e), j))

    pl.when(odd)(lambda: start_x(0).start())
    for e in hops:
        plane_x(e).start()
    for e in hops:
        start_x(e).start()
    own_copy().wait()

    @pl.when(even)
    def _():
        rc(h_ref, hw.at[i + 1], ks.at[0], xr.at[i + 1, 0], sibling).wait_recv()

        def cols(slot):
            for q in range(2):
                total = None
                for s in range(slabs):
                    term = bdot(hw[2 * p + q, s], hw[slot, s], NT)
                    total = term if total is None else total + term
                hi, lo = split(total)
                at = pl.ds(pl.multiple_of(slot * hrows, hrows), hrows)
                ghi[q * hrows : (q + 1) * hrows, at] = hi
                glo[q * hrows : (q + 1) * hrows, at] = lo

        def all_cols(slots):
            def step(t, carry):
                slot = slots[0]
                for u in range(1, len(slots)):
                    slot = jnp.where(t == u, slots[u], slot)
                cols(slot)
                return carry

            lax.fori_loop(0, len(slots), step, 0)

        for e in hops:
            for q in range(2):
                slot = 2 * source(e) + q
                rc(h_ref, hw.at[slot], ks.at[0], xr.at[slot, 0], sibling).wait_recv()
                if corner:
                    forward_x(e, q).start()
        all_cols([2 * p, 2 * p + 1] + [2 * source(e) + q for e in hops for q in range(2)])
        rc(bxc, begin.at[p, pl.ds(half, half)], ks.at[0], br.at[i + 1, 0], sibling).wait_recv()
        for e in hops:
            for q in range(2):
                pp = source(e)
                rc(bxc, begin.at[pp, pl.ds(q * half, half)], ks.at[0], br.at[2 * pp + q, 0], sibling).wait_recv()
                if corner:
                    forward_start(e, q).start()
        if corner:
            for q in range(2):
                slot = 2 * source(3) + q
                for b in range(2):
                    at = hw.at[slot, pl.ds(b * sh, sh)]
                    rc(at, at, ks.at[0], xr.at[slot, b], sibling).wait_recv()
            all_cols([2 * source(3), 2 * source(3) + 1])
            for q in range(2):
                for b in range(2):
                    at = begin.at[source(3), q * half + b]
                    rc(at, at, ks.at[0], br.at[2 * source(3) + q, b], sibling).wait_recv()

    def taken(s, first, last):
        return jnp.logical_or(jnp.logical_and(j == first, s > 1), jnp.logical_and(j == last, s < n - 2))

    def back_copies(to, s, b):
        at = pl.ds(pl.multiple_of(s * hcols + b * width, width), width)
        return [
            rc(src.at[s, :, pieces[b]], dst.at[:, at], gs.at[m, s, b], gr.at[m, s, b], (i, to))
            for m, (src, dst) in enumerate(((back_hi, ghi), (back_lo, glo)))
        ]

    @pl.when(odd)
    def _():
        for d in range(1, n):
            jj = mod(j - d)
            rc(begin.at[jj, p], begin.at[jj, p], bzs.at[0], bzr.at[d], sibling).wait_recv()
            for e in range(1, n):
                rc(begin.at[jj, p], begin.at[jj, p], bps.at[e, d], bpr.at[e, d], (2 * mod(p + e) + 1, j)).start()
        rc(h_ref, hw.at[j * 2], ks.at[0], yr.at[j * 2, 0], sibling).wait_recv()

        def cols(jj):
            total = None
            for q in range(2):
                for s in range(slabs):
                    term = bdot(hw[2 * j + q, s], hw[2 * jj + q, s], TN)
                    total = term if total is None else total + term
            hi, lo = split(total)
            at = pl.ds(pl.multiple_of(jj * hcols, hcols), hcols)
            ghi[:, at] = hi
            glo[:, at] = lo

        cols(j)

        def give_back(base, s, b):
            total = None
            for q in range(2):
                for t in range(slabs):
                    term = bdot(hw[2 * base + q, t], hw[2 * s + q, t, :, pieces[b]], TN)
                    total = term if total is None else total + term
            back_hi[s, :, pieces[b]], back_lo[s, :, pieces[b]] = split(total)
            for copy in back_copies(base, s, b):
                copy.start()

        def step(d, carry):
            low, high = jnp.maximum(j - d, 0), jnp.minimum(j + d, n - 1)
            from_low = jnp.logical_and(j - d >= 0, jnp.logical_or(d == 1, j < n - 1))
            from_high = jnp.logical_and(j + d < n, jnp.logical_or(d == 1, j > 0))
            for_first = jnp.logical_and(from_high, j == 1)
            for_last = jnp.logical_and(from_low, j == n - 2)
            for b in range(2):
                for q in range(2):
                    @pl.when(from_low)
                    def _():
                        s = low * 2 + q
                        right(hw.at[s], s, b).wait_recv()
                        pl.when(j < n - 2)(lambda: right(hw.at[s], s, b).start())

                    @pl.when(from_high)
                    def _():
                        s = high * 2 + q
                        left(hw.at[s], s, b).wait_recv()
                        pl.when(j > 1)(lambda: left(hw.at[s], s, b).start())

                pl.when(jnp.logical_and(for_first, d > 1))(lambda: give_back(0, high, b))
                pl.when(jnp.logical_and(for_last, d > 1))(lambda: give_back(n - 1, low, b))
            for b in range(2):
                pl.when(jnp.logical_and(for_first, d == 1))(lambda: give_back(0, high, b))
                pl.when(jnp.logical_and(for_last, d == 1))(lambda: give_back(n - 1, low, b))
            pl.when(from_low)(lambda: cols(low))
            pl.when(from_high)(lambda: cols(high))
            return carry

        lax.fori_loop(1, n, step, 0)
        for s in range(n):
            for b in range(2):
                @pl.when(taken(s, 0, n - 1))
                def _():
                    for copy in back_copies(j, s, b):
                        copy.wait_recv()

        for d in range(1, n):
            for e in range(1, n):
                at = begin.at[mod(j - d), mod(p - e)]
                rc(at, at, bzs.at[0], bpr.at[e, d], sibling).wait_recv()

    def reduce_copy(it, d):
        to = mod(r + d)
        return rc(part.at[it, to], rslots.at[it, d - 1], rs.at[it, d], rr.at[it, d], dev(a, to))

    def product(it):
        def block(to):
            at = pl.ds(pl.multiple_of(to * chunk, chunk), chunk)
            basis = bhi[...], blo[...]
            part[it, to] = dot3((ghi[at, :], glo[at, :]), basis, NN)

        for d in range(1, n):
            block(mod(r + d))
            reduce_copy(it, d).start()
        block(r)

    def spread_basis(source):
        def step(q, carry):
            at = pl.ds(pl.multiple_of(q * n * chunk, n * chunk), n * chunk)
            hi, lo = split(source(q).reshape(n * chunk, rank))
            bhi[at, :] = hi
            blo[at, :] = lo
            return carry

        lax.fori_loop(0, n, step, 0)

    def turned(it, turn):
        return lambda q: dot3(split(image[it, q].reshape(n * chunk, rank)), turn, NT)

    spread_basis(lambda q: begin[q])
    product(0)

    def line_copy(it, d, src_j, to_j):
        q, w = place(p, src_j)
        return rc(image.at[it, q, w], image.at[it, q, w], as_.at[it, d], ar.at[it, d], (i, to_j))

    def plane_copy(it, e, d):
        q, w = place(p, mod(j - d))
        return rc(image.at[it, q, w], image.at[it, q, w], ps.at[it, e, d], pr.at[it, e, d], (2 * peer(e) + c, j))

    def half_copy(it, e, d):
        q, w = place(source(e), mod(j - d))
        at = image.at[it, q, w, pl.ds((e - 1) * (chunk // 2), chunk // 2)]
        return rc(at, at, ps.at[it, 0 if e == 1 else 3, d], pr.at[it, 0 if e == 1 else 3, d], (2 * peer(3 - e) + c, j))

    def forward(it, d):
        if corner:
            for e in hops:
                q, w = place(source(e), mod(j - d))
                at = image.at[it, q, w]
                rc(at, at, ps.at[it, e, d], pr.at[it, e, d], sibling).wait_recv()
                half_copy(it, e, d).start()

    def arriving(it, e, d):
        q, w = place(source(e), mod(j - d))
        if not corner:
            return [(image.at[it, q, w], ps.at[it, e, d], pr.at[it, e, d])]
        return [
            (image.at[it, q, w, pl.ds(b * (chunk // 2), chunk // 2)], ps.at[it, 3 * b, d], pr.at[it, 3 * b, d])
            for b in range(2)
        ]

    def inner_one(it, e):
        to = mod(p + e)
        return rc(ipart.at[it, to], islots.at[it, e - 1], i1s.at[it, e], i1r.at[it, e], (2 * to + c, j))

    def inner_two(it, e):
        return rc(inner.at[it, p], inner.at[it, p], i2s.at[it, e], i2r.at[it, e], (2 * mod(p + e) + c, j))

    def iteration(it, carry):
        for d in range(1, n):
            reduce_copy(it, d).wait_recv()
        total = part[it, r]
        for d in range(1, n):
            total = total + rslots[it, d - 1]
        image[it, a, r] = total
        for d in range(1, n):
            line_copy(it, d, j, mod(j + d)).start()
        spread_needed = jnp.logical_or(odd, it < ITERS - 1)

        @pl.when(spread_needed)
        def _():
            for e in hops:
                plane_copy(it, e, 0).start()

        top, low = mul(total[:, :side], total, TN), mul(total[:, side:], total[:, side:], TN)
        for d in range(1, n):
            line_copy(it, d, mod(j - d), j).wait_recv()
            q, w = place(p, mod(j - d))
            rows = image[it, q, w]
            top = top + mul(rows[:, :side], rows, TN)
            low = low + mul(rows[:, side:], rows[:, side:], TN)
        ipart[it] = jnp.concatenate([top[:, :side], top[:, side:], low], axis=0).reshape(n, irows, side)
        for e in range(1, n):
            inner_one(it, e).start()
        pl.when(spread_needed)(lambda: forward(it, 0))
        for e in range(1, n):
            inner_one(it, e).wait_recv()
        total = ipart[it, p]
        for e in range(1, n):
            total = total + islots[it, e - 1]
        inner[it, p] = total
        for e in range(1, n):
            inner_two(it, e).start()

        @pl.when(spread_needed)
        def _():
            for d in range(1, n):
                for e in hops:
                    plane_copy(it, e, d).start()

        for e in range(1, n):
            at = inner.at[it, mod(p - e)]
            rc(at, at, i2s.at[it, e], i2r.at[it, e], sibling).wait_recv()

        def between(step, steps):
            for d in range(1, n):
                if min(d - 1, steps - 1) == step:
                    pl.when(spread_needed)(lambda: forward(it, d))

        flat = inner[it].reshape(3 * side, side)
        upper = flat[side : 2 * side]
        whole = jnp.concatenate([
            jnp.concatenate([flat[:side], upper], axis=1), jnp.concatenate([upper.T, flat[2 * side :]], axis=1),
        ], axis=0)
        inverse_factor(whole, work, linv, between)

        @pl.when(spread_needed)
        def _():
            for d in range(n):
                for e in far:
                    for at in arriving(it, e, d):
                        rc(at[0], at[0], at[1], at[2], sibling).wait_recv()


        @pl.when(it < ITERS - 1)
        def _():
            turn = split(linv[...])
            spread_basis(turned(it, turn))
            product(jnp.minimum(it + 1, ITERS - 1))

        for d in range(1, n):
            reduce_copy(it, d).wait_send()
            line_copy(it, d, j, mod(j + d)).wait_send()
        for e in range(1, n):
            inner_one(it, e).wait_send()
            inner_two(it, e).wait_send()

        @pl.when(spread_needed)
        def _():
            for d in range(n):
                for e in hops:
                    plane_copy(it, e, d).wait_send()
                    if corner:
                        half_copy(it, e, d).wait_send()

        return carry

    lax.fori_loop(0, ITERS, iteration, 0)

    last = ITERS - 1
    arows, bcols = out_ref.shape[1], out_ref.shape[2]
    give = rc(fxt, fxt, fs.at[0], fr.at[0], sibling)

    @pl.when(even)
    def _():
        turn = split(linv[...])
        rows = image[last, p].reshape(n * chunk, rank)
        fxt[...] = dot3(turn, split(rows), NT).astype(BF16)
        give.start()

    def part_copy(to):
        return rc(cpart.at[to], oslots.at[p], os_.at[to], or_.at[p], (to, j))

    middle = jnp.logical_and(j > 0, j < n - 1)
    work_here = jnp.logical_and(odd, middle)
    beside = jnp.logical_or(j == 1, j == n - 2)
    end = jnp.where(j <= 1, 0, n - 1)

    @pl.when(work_here)
    def _():
        mine = linv[pl.ds(pl.multiple_of(j * bcols, bcols), bcols), :]
        other = linv[pl.ds(pl.multiple_of(end * bcols, bcols), bcols), :]
        turn = split(jnp.concatenate([mine, other], axis=0))

        def step(q, carry):
            at = pl.ds(pl.multiple_of(q * n * chunk, n * chunk), n * chunk)
            fy[at, :] = turned(last, turn)(q).astype(BF16)
            return carry

        lax.fori_loop(0, n, step, 0)
        for q in range(2):
            for s in range(slabs):
                total = None
                for jj in range(n):
                    term = bdot(hw[2 * jj + q, s], fy[jj * hcols : (jj + 1) * hcols, :], NN)
                    total = term if total is None else total + term
                wsum[q, s] = total
        give.wait_recv()
        for s in range(slabs):
            total = None
            for q in range(2):
                tall = fxt[:, q * hrows : (q + 1) * hrows]
                hi, lo = split(wsum[q, s])
                term = bdot(tall, hi, NN) + bdot(tall, lo, NN)
                total = term if total is None else total + term
            for to in range(2 * n):
                cpart[to, s] = total[to * arows : (to + 1) * arows, :]
        for e in range(1, 2 * n):
            part_copy(lax.rem(i + e, 2 * n)).start()
        oslots[p] = cpart[i]

    pl.when(jnp.logical_and(odd, jnp.logical_not(middle)))(lambda: give.wait_recv())
    hand = rc(extra, final, es.at[0], er.at[0], (i, end))

    @pl.when(middle)
    def _():
        for pp in range(n):
            @pl.when(jnp.logical_or(even, p != pp))
            def _():
                rc(oslots.at[pp], oslots.at[pp], fs.at[0], or_.at[pp], sibling).wait_recv()

        total = oslots[0]
        for pp in range(1, n):
            total = total + oslots[pp]
        out_ref[...] = total[:, :, :bcols]
        extra[...] = total[:, :, bcols:]
        pl.when(beside)(lambda: hand.start())

    @pl.when(jnp.logical_not(middle))
    def _():
        hand.wait_recv()
        out_ref[...] = final[...]

    pl.when(even)(lambda: give.wait_send())
    pl.when(jnp.logical_and(middle, beside))(lambda: hand.wait_send())
    pl.when(even)(lambda: rc(h_ref, hw.at[ykey], ks.at[0], yr.at[ykey, 0], sibling).wait_send())
    pl.when(odd)(lambda: rc(h_ref, hw.at[i], ks.at[0], xr.at[i, 0], sibling).wait_send())
    pl.when(odd)(lambda: start_x(0).wait_send())
    for e in hops:
        plane_x(e).wait_send()
        start_x(e).wait_send()
    for b in range(2):
        pl.when(j < n - 1)(lambda: right(h_ref, ykey, b).wait_send())
        pl.when(j > 0)(lambda: left(h_ref, ykey, b).wait_send())

    if corner:
        @pl.when(even)
        def _():
            for e in hops:
                for q in range(2):
                    forward_x(e, q).wait_send()
                    forward_start(e, q).wait_send()

    @pl.when(work_here)
    def _():
        for e in range(1, 2 * n):
            part_copy(lax.rem(i + e, 2 * n)).wait_send()

    @pl.when(odd)
    def _():
        for d in range(1, n):
            rc(begin.at[j, p], begin.at[j, p], bzs.at[d], bzr.at[d], (i, mod(j + d))).wait_send()
            for e in range(1, n):
                at = begin.at[mod(j - d), p]
                rc(at, at, bps.at[e, d], bpr.at[e, d], (2 * mod(p + e) + 1, j)).wait_send()
        for s in range(n):
            for b in range(2):
                @pl.when(taken(s, 1, n - 2))
                def _():
                    for copy in back_copies(jnp.where(j == 1, 0, n - 1), s, b):
                        copy.wait_send()

        for d in range(1, n):
            for b in range(2):
                for q in range(2):
                    @pl.when(jnp.logical_and(j - d >= 0, j < n - 2))
                    def _():
                        s = jnp.maximum(j - d, 0) * 2 + q
                        right(hw.at[s], s, b).wait_send()

                    @pl.when(jnp.logical_and(j + d < n, j > 1))
                    def _():
                        s = jnp.minimum(j + d, n - 1) * 2 + q
                        left(hw.at[s], s, b).wait_send()


def on_device(history, start_x, start_y):
    nx, n = lax.axis_size("gx"), lax.axis_size("gy")
    slabs, hrows, hcols = history.shape
    rank = start_x.shape[1]
    rows = 2 * hrows
    assert nx == 2 * n and rows == hcols and n % 2 == 0 and n > 3 and slabs % 2 == 0
    chunk = rows // n
    dma = pltpu.SemaphoreType.DMA
    vmem = pltpu.VMEM
    arows, bcols = rank // nx, rank // n
    piece = (3 * (rank // 2) // n, rank // 2)
    shape, pair = (slabs, arows, bcols), (slabs, arows, 2 * bcols)
    scratch = [
        vmem((2 * n, slabs, hrows, hcols), BF16),
        vmem((rows, n * rows), BF16), vmem((rows, n * rows), BF16),
        vmem((n, n, chunk, rank), F32),
        vmem((n * rows, rank), BF16), vmem((n * rows, rank), BF16),
        vmem((ITERS, n, chunk, rank), F32),
        vmem((ITERS, n - 1, chunk, rank), F32),
        vmem((ITERS, n, n, chunk, rank), F32),
        vmem((ITERS, n) + piece, F32),
        vmem((ITERS, n - 1) + piece, F32),
        vmem((ITERS, n) + piece, F32),
        vmem((rank, 2 * rank), F32),
        vmem((rank, rank), F32),
        vmem((rank, rows), BF16),
        vmem((n * rows, 2 * bcols), BF16),
        vmem((2, slabs, hrows, 2 * bcols), F32),
        vmem((nx,) + pair, F32),
        vmem((n,) + pair, F32),
        vmem((n, rows, hcols), BF16), vmem((n, rows, hcols), BF16),
        vmem(shape, F32), vmem(shape, F32),
        dma((1,)),
        dma((n,)), dma((nx, 2)),
        dma((n,)), dma((n,)),
        dma((n, n)), dma((n, n)),
        dma((n,)), dma((nx, 2)),
        dma((nx, 2)), dma((nx, 2)), dma((1,)), dma((nx, 2)),
        dma((ITERS, n)), dma((ITERS, n)),
        dma((ITERS, n)), dma((ITERS, n)),
        dma((ITERS, n, n)), dma((ITERS, n, n)),
        dma((ITERS, n)), dma((ITERS, n)),
        dma((ITERS, n)), dma((ITERS, n)),
        dma((1,)), dma((1,)),
        dma((nx,)), dma((n,)),
        dma((3, 2)), dma((3, 2)),
        dma((2, n, 2)), dma((2, n, 2)),
        dma((1,)), dma((1,)),
    ]
    return pl.pallas_call(
        functools.partial(kernel, n),
        out_shape=jax.ShapeDtypeStruct(shape, F32),
        in_specs=[pl.BlockSpec(memory_space=pl.ANY)] + [pl.BlockSpec(memory_space=pltpu.VMEM)] * 2,
        out_specs=pl.BlockSpec(memory_space=pltpu.VMEM),
        scratch_shapes=scratch,
        compiler_params=pltpu.CompilerParams(
            collective_id=0, has_side_effects=True, vmem_limit_bytes=56 * 1024 * 1024
        ),
        name="tucker",
    )(history, start_x, start_y)


def solution(mesh):
    return jax.shard_map(
        on_device,
        mesh=mesh,
        in_specs=(P(None, "gx", "gy"), P("gx", None), P("gy", None)),
        out_specs=P(None, "gx", "gy"),
        check_vma=False,
    )
```

```python
import functools

import jax
import jax.numpy as jnp
from jax import lax
from jax.experimental import pallas as pl
from jax.experimental.pallas import tpu as pltpu
from jax.sharding import PartitionSpec as P

ITERS = 3
BLOCK = 64
HIGHEST = lax.Precision.HIGHEST
MESH = pl.DeviceIdType.MESH
F32, BF16 = jnp.float32, jnp.bfloat16
NN, NT, TN = ((1,), (0,)), ((1,), (1,)), ((0,), (0,))


def mul(a, b, dims):
    return lax.dot_general(a, b, (dims, ((), ())), precision=HIGHEST, preferred_element_type=F32)


def bdot(a, b, dims):
    return lax.dot_general(a, b, (dims, ((), ())), preferred_element_type=F32)


def split(v):
    hi = v.astype(BF16)
    return hi, (v - hi.astype(F32)).astype(BF16)


def dot3(a, b, dims):
    return bdot(a[0], b[0], dims) + (bdot(a[0], b[1], dims) + bdot(a[1], b[0], dims))


def eliminate(block):
    size = block.shape[0]
    sub = lax.broadcasted_iota(jnp.int32, (size, size), 0)
    lane = lax.broadcasted_iota(jnp.int32, (size, size), 1)
    eye = jnp.where(sub == lane, 1.0, 0.0).astype(F32)
    full = (8, 2 * size)
    sub8 = lax.broadcasted_iota(jnp.int32, full, 0)
    whole = jnp.concatenate([block, eye], axis=1)
    rows = [whole[t * 8 : t * 8 + 8] for t in range(size // 8)]
    for home in range(size // 8):
        k = home * 8
        tiles = range(home, size // 8)
        cols = {t: [jnp.broadcast_to(rows[t][:, k + m : k + m + 1], full) for m in range(8)] for t in tiles}
        piv = [[jnp.broadcast_to(cols[home][l][m : m + 1, :], full) for l in range(8)] for m in range(8)]
        held = [jnp.broadcast_to(rows[home][m : m + 1, :], full) for m in range(8)]
        inv = []
        for m in range(0, 8, 2):
            first, cross, second = piv[m][m], piv[m][m + 1], piv[m + 1][m + 1]
            inv0 = 1.0 / first
            inv1 = first * (1.0 / (first * second - cross * cross))
            ratio = cross * inv0
            inv += [inv0, inv1]
            held[m + 1] = held[m + 1] - ratio * held[m]
            for t in tiles:
                cols[t][m + 1] = cols[t][m + 1] - ratio * cols[t][m]
            for l in range(m + 2, 8):
                piv[m + 1][l] = piv[m + 1][l] - ratio * piv[m][l]
            for q in range(m + 2, 8):
                by0, by1 = piv[m][q] * inv0, piv[m + 1][q] * inv1
                for l in range(q, 8):
                    piv[q][l] = piv[q][l] - by0 * piv[m][l] - by1 * piv[m + 1][l]
                held[q] = held[q] - by0 * held[m] - by1 * held[m + 1]
                for t in tiles:
                    cols[t][q] = cols[t][q] - by0 * cols[t][m] - by1 * cols[t][m + 1]
        scaled = [held[m] * inv[m] for m in range(8)]
        for t in tiles:
            for m in range(8):
                col = cols[t][m]
                if t == home:
                    if m == 7:
                        continue
                    col = jnp.where(sub8 > m, col, 0.0)
                rows[t] = rows[t] - col * scaled[m]
    whole = jnp.concatenate(rows, axis=0)
    diag = jnp.sum(jnp.where(sub == lane, whole[:, :size], 0.0), axis=1, keepdims=True)
    return whole[:, size:] * (1.0 / jnp.sqrt(diag))


def inverse_factor(inner, work, out_ref, between):
    rank = inner.shape[0]
    sub = lax.broadcasted_iota(jnp.int32, (rank, rank), 0)
    lane = lax.broadcasted_iota(jnp.int32, (rank, rank), 1)
    same = sub == lane
    diag = jnp.where(same, inner, 0.0)
    tall = 1.0 / jnp.sqrt(jnp.sum(diag, axis=1, keepdims=True))
    wide = 1.0 / jnp.sqrt(jnp.sum(diag, axis=0, keepdims=True))
    work[:, :rank] = inner * tall * wide
    work[:, rank:] = jnp.where(same, 1.0, 0.0).astype(F32)
    for step, at in enumerate(range(0, rank, BLOCK)):
        inverse = eliminate(work[at : at + BLOCK, at : at + BLOCK])
        top = mul(inverse, work[at : at + BLOCK, :], NN)
        out_ref[at : at + BLOCK, :] = top[:, rank:] * wide
        if at + BLOCK < rank:
            left = top[:, at + BLOCK : rank]
            work[at + BLOCK :, :] = work[at + BLOCK :, :] - mul(left, top, TN)
        between(step, rank // BLOCK)


def kernel(
    n, h_ref, bx_ref, by_ref, out_ref,
    hw, ghi, glo, begin, bhi, blo, part, rslots, image, ipart, islots, inner, work, linv, fxt, fy, wsum, cpart, oslots, back_hi, back_lo, extra, final,
    own, bs, br, bzs, bzr, bps, bpr, xs, xr, zr, zl, ks, yr, rs, rr, as_, ar, ps, pr, i1s, i1r, i2s, i2r, fs, fr, os_, or_, fxs, fbs, gs, gr, es, er,
):
    i, j = lax.axis_index("gx"), lax.axis_index("gy")
    p, c = i // 2, lax.rem(i, 2)
    even = c == 0
    odd = c == 1
    slabs, hrows, hcols = h_ref.shape
    rank = bx_ref.shape[1]
    chunk = image.shape[3]
    side = rank // 2
    irows = 3 * side // n
    sibling = (i + 1 - 2 * c, j)

    def mod(v):
        return lax.rem(v + n, n)

    def rc(src, dst, ss, rsem, dev):
        return pltpu.make_async_remote_copy(
            src_ref=src, dst_ref=dst, send_sem=ss, recv_sem=rsem, device_id=dev, device_id_type=MESH
        )

    a = jnp.where(even, p, j)
    r = jnp.where(even, j, p)

    def dev(aa, rr_):
        return (jnp.where(even, 2 * aa, 2 * rr_ + 1), jnp.where(even, rr_, aa))

    def place(pp, jj):
        return jnp.where(even, pp, jj), jnp.where(even, jj, pp)

    corner = n == 4
    hops = (1, 2) if corner else tuple(range(1, n))
    far = (3,) if corner else hops

    def across(e):
        return (p + 1 - 2 * lax.rem(p, 2), lax.rem(p + 2, n), n - 1 - p)[e - 1]

    def peer(e):
        return across(e) if corner else mod(p + e)

    def source(e):
        return across(e) if corner else mod(p - e)

    barrier = pltpu.get_barrier_semaphore()
    for e in range(1, 2 * n):
        pl.semaphore_signal(barrier, inc=1, device_id=(lax.rem(i + e, 2 * n), j), device_id_type=MESH)
    for d in range(1, n):
        for cc in range(2):
            pl.semaphore_signal(barrier, inc=1, device_id=(2 * p + cc, mod(j + d)), device_id_type=MESH)
    pl.semaphore_wait(barrier, 2 * n - 1 + 2 * (n - 1))

    @pl.when(even)
    def _():
        for q in range(n // 2):
            begin[p, q] = bx_ref[q * chunk : (q + 1) * chunk, :]

    @pl.when(odd)
    def _():
        for q in range(n):
            begin[j, q] = by_ref[q * chunk : (q + 1) * chunk, :]
        for d in range(1, n):
            rc(begin.at[j, p], begin.at[j, p], bzs.at[d], bzr.at[d], (i, mod(j + d))).start()

    ykey = j * 2 + c

    width = hcols // 2
    pieces = [pl.ds(b * width, width) for b in range(2)]

    def right(src, s, b):
        to = (2 * p + 1, jnp.minimum(j + 1, n - 1))
        return rc(src.at[:, :, pieces[b]], hw.at[s, :, :, pieces[b]], zr.at[s, b], yr.at[s, b], to)

    def left(src, s, b):
        to = (2 * p + 1, jnp.maximum(j - 1, 0))
        return rc(src.at[:, :, pieces[b]], hw.at[s, :, :, pieces[b]], zl.at[s, b], yr.at[s, b], to)

    for b in range(2):
        pl.when(j < n - 1)(lambda: right(h_ref, ykey, b).start())
        pl.when(j > 0)(lambda: left(h_ref, ykey, b).start())

    def own_copy():
        return pltpu.make_async_copy(h_ref, hw.at[jnp.where(even, i, ykey)], own.at[0])

    own_copy().start()
    pl.when(even)(lambda: rc(h_ref, hw.at[ykey], ks.at[0], yr.at[ykey, 0], sibling).start())
    pl.when(odd)(lambda: rc(h_ref, hw.at[i], ks.at[0], xr.at[i, 0], sibling).start())

    half = n // 2

    bxc = bx_ref.reshape(half, chunk, rank)

    def start_x(e):
        dst = begin.at[p, pl.ds(c * half, half)]
        return rc(bxc, dst, bs.at[e], br.at[i, 0], (2 * (p if e == 0 else peer(e)), j))

    def plane_x(e):
        return rc(h_ref, hw.at[i], xs.at[e], xr.at[i, 0], (2 * peer(e), j))

    sh = slabs // 2

    def forward_x(e, q):
        slot = 2 * source(e) + q
        at = hw.at[slot, pl.ds((e - 1) * sh, sh)]
        return rc(at, at, fxs.at[e, q], xr.at[slot, e - 1], (2 * peer(3 - e), j))

    def forward_start(e, q):
        at = begin.at[source(e), q * half + e - 1]
        return rc(at, at, fbs.at[e, q], br.at[2 * source(e) + q, e - 1], (2 * peer(3 - e), j))

    pl.when(odd)(lambda: start_x(0).start())
    for e in hops:
        plane_x(e).start()
    for e in hops:
        start_x(e).start()
    own_copy().wait()

    @pl.when(even)
    def _():
        rc(h_ref, hw.at[i + 1], ks.at[0], xr.at[i + 1, 0], sibling).wait_recv()

        def cols(slot):
            for q in range(2):
                total = None
                for s in range(slabs):
                    term = bdot(hw[2 * p + q, s], hw[slot, s], NT)
                    total = term if total is None else total + term
                hi, lo = split(total)
                at = pl.ds(pl.multiple_of(slot * hrows, hrows), hrows)
                ghi[q * hrows : (q + 1) * hrows, at] = hi
                glo[q * hrows : (q + 1) * hrows, at] = lo

        def all_cols(slots):
            def step(t, carry):
                slot = slots[0]
                for u in range(1, len(slots)):
                    slot = jnp.where(t == u, slots[u], slot)
                cols(slot)
                return carry

            lax.fori_loop(0, len(slots), step, 0)

        for e in hops:
            for q in range(2):
                slot = 2 * source(e) + q
                rc(h_ref, hw.at[slot], ks.at[0], xr.at[slot, 0], sibling).wait_recv()
                if corner:
                    forward_x(e, q).start()
        all_cols([2 * p, 2 * p + 1] + [2 * source(e) + q for e in hops for q in range(2)])
        rc(bxc, begin.at[p, pl.ds(half, half)], ks.at[0], br.at[i + 1, 0], sibling).wait_recv()
        for e in hops:
            for q in range(2):
                pp = source(e)
                rc(bxc, begin.at[pp, pl.ds(q * half, half)], ks.at[0], br.at[2 * pp + q, 0], sibling).wait_recv()
                if corner:
                    forward_start(e, q).start()
        if corner:
            for q in range(2):
                slot = 2 * source(3) + q
                for b in range(2):
                    at = hw.at[slot, pl.ds(b * sh, sh)]
                    rc(at, at, ks.at[0], xr.at[slot, b], sibling).wait_recv()
            all_cols([2 * source(3), 2 * source(3) + 1])
            for q in range(2):
                for b in range(2):
                    at = begin.at[source(3), q * half + b]
                    rc(at, at, ks.at[0], br.at[2 * source(3) + q, b], sibling).wait_recv()

    def taken(s, first, last):
        return jnp.logical_or(jnp.logical_and(j == first, s > 1), jnp.logical_and(j == last, s < n - 2))

    def back_copies(to, s, b):
        at = pl.ds(pl.multiple_of(s * hcols + b * width, width), width)
        return [
            rc(src.at[s, :, pieces[b]], dst.at[:, at], gs.at[m, s, b], gr.at[m, s, b], (i, to))
            for m, (src, dst) in enumerate(((back_hi, ghi), (back_lo, glo)))
        ]

    @pl.when(odd)
    def _():
        for d in range(1, n):
            jj = mod(j - d)
            rc(begin.at[jj, p], begin.at[jj, p], bzs.at[0], bzr.at[d], sibling).wait_recv()
            for e in range(1, n):
                rc(begin.at[jj, p], begin.at[jj, p], bps.at[e, d], bpr.at[e, d], (2 * mod(p + e) + 1, j)).start()
        rc(h_ref, hw.at[j * 2], ks.at[0], yr.at[j * 2, 0], sibling).wait_recv()

        def cols(jj):
            total = None
            for q in range(2):
                for s in range(slabs):
                    term = bdot(hw[2 * j + q, s], hw[2 * jj + q, s], TN)
                    total = term if total is None else total + term
            hi, lo = split(total)
            at = pl.ds(pl.multiple_of(jj * hcols, hcols), hcols)
            ghi[:, at] = hi
            glo[:, at] = lo

        cols(j)

        def give_back(base, s, b):
            total = None
            for q in range(2):
                for t in range(slabs):
                    term = bdot(hw[2 * base + q, t], hw[2 * s + q, t, :, pieces[b]], TN)
                    total = term if total is None else total + term
            back_hi[s, :, pieces[b]], back_lo[s, :, pieces[b]] = split(total)
            for copy in back_copies(base, s, b):
                copy.start()

        def step(d, carry):
            low, high = jnp.maximum(j - d, 0), jnp.minimum(j + d, n - 1)
            from_low = jnp.logical_and(j - d >= 0, jnp.logical_or(d == 1, j < n - 1))
            from_high = jnp.logical_and(j + d < n, jnp.logical_or(d == 1, j > 0))
            for_first = jnp.logical_and(from_high, j == 1)
            for_last = jnp.logical_and(from_low, j == n - 2)
            for b in range(2):
                for q in range(2):
                    @pl.when(from_low)
                    def _():
                        s = low * 2 + q
                        right(hw.at[s], s, b).wait_recv()
                        pl.when(j < n - 2)(lambda: right(hw.at[s], s, b).start())

                    @pl.when(from_high)
                    def _():
                        s = high * 2 + q
                        left(hw.at[s], s, b).wait_recv()
                        pl.when(j > 1)(lambda: left(hw.at[s], s, b).start())

                pl.when(jnp.logical_and(for_first, d > 1))(lambda: give_back(0, high, b))
                pl.when(jnp.logical_and(for_last, d > 1))(lambda: give_back(n - 1, low, b))
            for b in range(2):
                pl.when(jnp.logical_and(for_first, d == 1))(lambda: give_back(0, high, b))
                pl.when(jnp.logical_and(for_last, d == 1))(lambda: give_back(n - 1, low, b))
            pl.when(from_low)(lambda: cols(low))
            pl.when(from_high)(lambda: cols(high))
            return carry

        lax.fori_loop(1, n, step, 0)
        for s in range(n):
            for b in range(2):
                @pl.when(taken(s, 0, n - 1))
                def _():
                    for copy in back_copies(j, s, b):
                        copy.wait_recv()

        for d in range(1, n):
            for e in range(1, n):
                at = begin.at[mod(j - d), mod(p - e)]
                rc(at, at, bzs.at[0], bpr.at[e, d], sibling).wait_recv()

    def reduce_copy(it, d):
        to = mod(r + d)
        return rc(part.at[it, to], rslots.at[it, d - 1], rs.at[it, d], rr.at[it, d], dev(a, to))

    def product(it):
        def block(to):
            at = pl.ds(pl.multiple_of(to * chunk, chunk), chunk)
            basis = bhi[...], blo[...]
            part[it, to] = dot3((ghi[at, :], glo[at, :]), basis, NN)

        for d in range(1, n):
            block(mod(r + d))
            reduce_copy(it, d).start()
        block(r)

    def spread_basis(source):
        def step(q, carry):
            at = pl.ds(pl.multiple_of(q * n * chunk, n * chunk), n * chunk)
            hi, lo = split(source(q).reshape(n * chunk, rank))
            bhi[at, :] = hi
            blo[at, :] = lo
            return carry

        lax.fori_loop(0, n, step, 0)

    def turned(it, turn):
        return lambda q: dot3(split(image[it, q].reshape(n * chunk, rank)), turn, NT)

    spread_basis(lambda q: begin[q])
    product(0)

    def line_copy(it, d, src_j, to_j):
        q, w = place(p, src_j)
        return rc(image.at[it, q, w], image.at[it, q, w], as_.at[it, d], ar.at[it, d], (i, to_j))

    def plane_copy(it, e, d):
        q, w = place(p, mod(j - d))
        return rc(image.at[it, q, w], image.at[it, q, w], ps.at[it, e, d], pr.at[it, e, d], (2 * peer(e) + c, j))

    def start_plane(it, d):
        @pl.when(even)
        def _():
            for e in hops:
                plane_copy(it, e, d).start()

        @pl.when(odd)
        def _():
            for e in reversed(hops):
                plane_copy(it, e, d).start()

    def half_copy(it, e, d):
        q, w = place(source(e), mod(j - d))
        at = image.at[it, q, w, pl.ds((e - 1) * (chunk // 2), chunk // 2)]
        return rc(at, at, ps.at[it, 0 if e == 1 else 3, d], pr.at[it, 0 if e == 1 else 3, d], (2 * peer(3 - e) + c, j))

    def forward(it, d):
        if corner:
            for e in hops:
                q, w = place(source(e), mod(j - d))
                at = image.at[it, q, w]
                rc(at, at, ps.at[it, e, d], pr.at[it, e, d], sibling).wait_recv()
                half_copy(it, e, d).start()

    def arriving(it, e, d):
        q, w = place(source(e), mod(j - d))
        if not corner:
            return [(image.at[it, q, w], ps.at[it, e, d], pr.at[it, e, d])]
        return [
            (image.at[it, q, w, pl.ds(b * (chunk // 2), chunk // 2)], ps.at[it, 3 * b, d], pr.at[it, 3 * b, d])
            for b in range(2)
        ]

    def inner_one(it, e):
        to = mod(p + e)
        return rc(ipart.at[it, to], islots.at[it, e - 1], i1s.at[it, e], i1r.at[it, e], (2 * to + c, j))

    def inner_two(it, e):
        return rc(inner.at[it, p], inner.at[it, p], i2s.at[it, e], i2r.at[it, e], (2 * mod(p + e) + c, j))

    def iteration(it, carry):
        for d in range(1, n):
            reduce_copy(it, d).wait_recv()
        total = part[it, r]
        for d in range(1, n):
            total = total + rslots[it, d - 1]
        image[it, a, r] = total
        for d in range(1, n):
            line_copy(it, d, j, mod(j + d)).start()
        spread_needed = jnp.logical_or(odd, it < ITERS - 1)

        @pl.when(spread_needed)
        def _():
            start_plane(it, 0)

        top, low = mul(total[:, :side], total, TN), mul(total[:, side:], total[:, side:], TN)
        for d in range(1, n):
            line_copy(it, d, mod(j - d), j).wait_recv()
            q, w = place(p, mod(j - d))
            rows = image[it, q, w]
            top = top + mul(rows[:, :side], rows, TN)
            low = low + mul(rows[:, side:], rows[:, side:], TN)
        ipart[it] = jnp.concatenate([top[:, :side], top[:, side:], low], axis=0).reshape(n, irows, side)
        for e in range(1, n):
            inner_one(it, e).start()
        pl.when(spread_needed)(lambda: forward(it, 0))
        for e in range(1, n):
            inner_one(it, e).wait_recv()
        total = ipart[it, p]
        for e in range(1, n):
            total = total + islots[it, e - 1]
        inner[it, p] = total
        for e in range(1, n):
            inner_two(it, e).start()

        @pl.when(spread_needed)
        def _():
            for d in range(1, n):
                start_plane(it, d)

        for e in range(1, n):
            at = inner.at[it, mod(p - e)]
            rc(at, at, i2s.at[it, e], i2r.at[it, e], sibling).wait_recv()

        def between(step, steps):
            for d in range(1, n):
                if min(d - 1, steps - 1) == step:
                    pl.when(spread_needed)(lambda: forward(it, d))

        flat = inner[it].reshape(3 * side, side)
        upper = flat[side : 2 * side]
        whole = jnp.concatenate([
            jnp.concatenate([flat[:side], upper], axis=1), jnp.concatenate([upper.T, flat[2 * side :]], axis=1),
        ], axis=0)
        inverse_factor(whole, work, linv, between)

        @pl.when(spread_needed)
        def _():
            for d in range(n):
                for e in far:
                    for at in arriving(it, e, d):
                        rc(at[0], at[0], at[1], at[2], sibling).wait_recv()


        @pl.when(it < ITERS - 1)
        def _():
            turn = split(linv[...])
            spread_basis(turned(it, turn))
            product(jnp.minimum(it + 1, ITERS - 1))

        for d in range(1, n):
            reduce_copy(it, d).wait_send()
            line_copy(it, d, j, mod(j + d)).wait_send()
        for e in range(1, n):
            inner_one(it, e).wait_send()
            inner_two(it, e).wait_send()

        @pl.when(spread_needed)
        def _():
            for d in range(n):
                for e in hops:
                    plane_copy(it, e, d).wait_send()
                    if corner:
                        half_copy(it, e, d).wait_send()

        return carry

    lax.fori_loop(0, ITERS, iteration, 0)

    last = ITERS - 1
    arows, bcols = out_ref.shape[1], out_ref.shape[2]
    give = rc(fxt, fxt, fs.at[0], fr.at[0], sibling)

    @pl.when(even)
    def _():
        turn = split(linv[...])
        rows = image[last, p].reshape(n * chunk, rank)
        fxt[...] = dot3(turn, split(rows), NT).astype(BF16)
        give.start()

    def part_copy(to):
        return rc(cpart.at[to], oslots.at[p], os_.at[to], or_.at[p], (to, j))

    middle = jnp.logical_and(j > 0, j < n - 1)
    work_here = jnp.logical_and(odd, middle)
    beside = jnp.logical_or(j == 1, j == n - 2)
    end = jnp.where(j <= 1, 0, n - 1)

    @pl.when(work_here)
    def _():
        mine = linv[pl.ds(pl.multiple_of(j * bcols, bcols), bcols), :]
        other = linv[pl.ds(pl.multiple_of(end * bcols, bcols), bcols), :]
        turn = split(jnp.concatenate([mine, other], axis=0))

        def step(q, carry):
            at = pl.ds(pl.multiple_of(q * n * chunk, n * chunk), n * chunk)
            fy[at, :] = turned(last, turn)(q).astype(BF16)
            return carry

        lax.fori_loop(0, n, step, 0)
        for q in range(2):
            for s in range(slabs):
                total = None
                for jj in range(n):
                    term = bdot(hw[2 * jj + q, s], fy[jj * hcols : (jj + 1) * hcols, :], NN)
                    total = term if total is None else total + term
                wsum[q, s] = total
        give.wait_recv()
        for s in range(slabs):
            total = None
            for q in range(2):
                tall = fxt[:, q * hrows : (q + 1) * hrows]
                hi, lo = split(wsum[q, s])
                term = bdot(tall, hi, NN) + bdot(tall, lo, NN)
                total = term if total is None else total + term
            for to in range(2 * n):
                cpart[to, s] = total[to * arows : (to + 1) * arows, :]
        for e in range(1, 2 * n):
            part_copy(lax.rem(i + e, 2 * n)).start()
        oslots[p] = cpart[i]

    pl.when(jnp.logical_and(odd, jnp.logical_not(middle)))(lambda: give.wait_recv())
    hand = rc(extra, final, es.at[0], er.at[0], (i, end))

    @pl.when(middle)
    def _():
        for pp in range(n):
            @pl.when(jnp.logical_or(even, p != pp))
            def _():
                rc(oslots.at[pp], oslots.at[pp], fs.at[0], or_.at[pp], sibling).wait_recv()

        total = oslots[0]
        for pp in range(1, n):
            total = total + oslots[pp]
        out_ref[...] = total[:, :, :bcols]
        extra[...] = total[:, :, bcols:]
        pl.when(beside)(lambda: hand.start())

    @pl.when(jnp.logical_not(middle))
    def _():
        hand.wait_recv()
        out_ref[...] = final[...]

    pl.when(even)(lambda: give.wait_send())
    pl.when(jnp.logical_and(middle, beside))(lambda: hand.wait_send())
    pl.when(even)(lambda: rc(h_ref, hw.at[ykey], ks.at[0], yr.at[ykey, 0], sibling).wait_send())
    pl.when(odd)(lambda: rc(h_ref, hw.at[i], ks.at[0], xr.at[i, 0], sibling).wait_send())
    pl.when(odd)(lambda: start_x(0).wait_send())
    for e in hops:
        plane_x(e).wait_send()
        start_x(e).wait_send()
    for b in range(2):
        pl.when(j < n - 1)(lambda: right(h_ref, ykey, b).wait_send())
        pl.when(j > 0)(lambda: left(h_ref, ykey, b).wait_send())

    if corner:
        @pl.when(even)
        def _():
            for e in hops:
                for q in range(2):
                    forward_x(e, q).wait_send()
                    forward_start(e, q).wait_send()

    @pl.when(work_here)
    def _():
        for e in range(1, 2 * n):
            part_copy(lax.rem(i + e, 2 * n)).wait_send()

    @pl.when(odd)
    def _():
        for d in range(1, n):
            rc(begin.at[j, p], begin.at[j, p], bzs.at[d], bzr.at[d], (i, mod(j + d))).wait_send()
            for e in range(1, n):
                at = begin.at[mod(j - d), p]
                rc(at, at, bps.at[e, d], bpr.at[e, d], (2 * mod(p + e) + 1, j)).wait_send()
        for s in range(n):
            for b in range(2):
                @pl.when(taken(s, 1, n - 2))
                def _():
                    for copy in back_copies(jnp.where(j == 1, 0, n - 1), s, b):
                        copy.wait_send()

        for d in range(1, n):
            for b in range(2):
                for q in range(2):
                    @pl.when(jnp.logical_and(j - d >= 0, j < n - 2))
                    def _():
                        s = jnp.maximum(j - d, 0) * 2 + q
                        right(hw.at[s], s, b).wait_send()

                    @pl.when(jnp.logical_and(j + d < n, j > 1))
                    def _():
                        s = jnp.minimum(j + d, n - 1) * 2 + q
                        left(hw.at[s], s, b).wait_send()


def on_device(history, start_x, start_y):
    nx, n = lax.axis_size("gx"), lax.axis_size("gy")
    slabs, hrows, hcols = history.shape
    rank = start_x.shape[1]
    rows = 2 * hrows
    assert nx == 2 * n and rows == hcols and n % 2 == 0 and n > 3 and slabs % 2 == 0
    chunk = rows // n
    dma = pltpu.SemaphoreType.DMA
    vmem = pltpu.VMEM
    arows, bcols = rank // nx, rank // n
    piece = (3 * (rank // 2) // n, rank // 2)
    shape, pair = (slabs, arows, bcols), (slabs, arows, 2 * bcols)
    scratch = [
        vmem((2 * n, slabs, hrows, hcols), BF16),
        vmem((rows, n * rows), BF16), vmem((rows, n * rows), BF16),
        vmem((n, n, chunk, rank), F32),
        vmem((n * rows, rank), BF16), vmem((n * rows, rank), BF16),
        vmem((ITERS, n, chunk, rank), F32),
        vmem((ITERS, n - 1, chunk, rank), F32),
        vmem((ITERS, n, n, chunk, rank), F32),
        vmem((ITERS, n) + piece, F32),
        vmem((ITERS, n - 1) + piece, F32),
        vmem((ITERS, n) + piece, F32),
        vmem((rank, 2 * rank), F32),
        vmem((rank, rank), F32),
        vmem((rank, rows), BF16),
        vmem((n * rows, 2 * bcols), BF16),
        vmem((2, slabs, hrows, 2 * bcols), F32),
        vmem((nx,) + pair, F32),
        vmem((n,) + pair, F32),
        vmem((n, rows, hcols), BF16), vmem((n, rows, hcols), BF16),
        vmem(shape, F32), vmem(shape, F32),
        dma((1,)),
        dma((n,)), dma((nx, 2)),
        dma((n,)), dma((n,)),
        dma((n, n)), dma((n, n)),
        dma((n,)), dma((nx, 2)),
        dma((nx, 2)), dma((nx, 2)), dma((1,)), dma((nx, 2)),
        dma((ITERS, n)), dma((ITERS, n)),
        dma((ITERS, n)), dma((ITERS, n)),
        dma((ITERS, n, n)), dma((ITERS, n, n)),
        dma((ITERS, n)), dma((ITERS, n)),
        dma((ITERS, n)), dma((ITERS, n)),
        dma((1,)), dma((1,)),
        dma((nx,)), dma((n,)),
        dma((3, 2)), dma((3, 2)),
        dma((2, n, 2)), dma((2, n, 2)),
        dma((1,)), dma((1,)),
    ]
    return pl.pallas_call(
        functools.partial(kernel, n),
        out_shape=jax.ShapeDtypeStruct(shape, F32),
        in_specs=[pl.BlockSpec(memory_space=pl.ANY)] + [pl.BlockSpec(memory_space=pltpu.VMEM)] * 2,
        out_specs=pl.BlockSpec(memory_space=pltpu.VMEM),
        scratch_shapes=scratch,
        compiler_params=pltpu.CompilerParams(
            collective_id=0, has_side_effects=True, vmem_limit_bytes=56 * 1024 * 1024
        ),
        name="tucker",
    )(history, start_x, start_y)


def solution(mesh):
    return jax.shard_map(
        on_device,
        mesh=mesh,
        in_specs=(P(None, "gx", "gy"), P("gx", None), P("gy", None)),
        out_specs=P(None, "gx", "gy"),
        check_vma=False,
    )
```

```python
import functools

import jax
import jax.numpy as jnp
from jax import lax
from jax.experimental import pallas as pl
from jax.experimental.pallas import tpu as pltpu
from jax.sharding import PartitionSpec as P

ITERS = 3
BLOCK = 64
HIGHEST = lax.Precision.HIGHEST
MESH = pl.DeviceIdType.MESH
F32, BF16 = jnp.float32, jnp.bfloat16
NN, NT, TN = ((1,), (0,)), ((1,), (1,)), ((0,), (0,))


def mul(a, b, dims):
    return lax.dot_general(a, b, (dims, ((), ())), precision=HIGHEST, preferred_element_type=F32)


def bdot(a, b, dims):
    return lax.dot_general(a, b, (dims, ((), ())), preferred_element_type=F32)


def split(v):
    hi = v.astype(BF16)
    return hi, (v - hi.astype(F32)).astype(BF16)


def dot3(a, b, dims):
    return bdot(a[0], b[0], dims) + (bdot(a[0], b[1], dims) + bdot(a[1], b[0], dims))


def eliminate(block):
    size = block.shape[0]
    sub = lax.broadcasted_iota(jnp.int32, (size, size), 0)
    lane = lax.broadcasted_iota(jnp.int32, (size, size), 1)
    eye = jnp.where(sub == lane, 1.0, 0.0).astype(F32)
    full = (8, 2 * size)
    sub8 = lax.broadcasted_iota(jnp.int32, full, 0)
    whole = jnp.concatenate([block, eye], axis=1)
    rows = [whole[t * 8 : t * 8 + 8] for t in range(size // 8)]
    for home in range(size // 8):
        k = home * 8
        tiles = range(home, size // 8)
        cols = {t: [jnp.broadcast_to(rows[t][:, k + m : k + m + 1], full) for m in range(8)] for t in tiles}
        piv = [[jnp.broadcast_to(cols[home][l][m : m + 1, :], full) for l in range(8)] for m in range(8)]
        held = [jnp.broadcast_to(rows[home][m : m + 1, :], full) for m in range(8)]
        inv = []
        for m in range(0, 8, 2):
            first, cross, second = piv[m][m], piv[m][m + 1], piv[m + 1][m + 1]
            inv0 = 1.0 / first
            inv1 = first * (1.0 / (first * second - cross * cross))
            ratio = cross * inv0
            inv += [inv0, inv1]
            held[m + 1] = held[m + 1] - ratio * held[m]
            for t in tiles:
                cols[t][m + 1] = cols[t][m + 1] - ratio * cols[t][m]
            for l in range(m + 2, 8):
                piv[m + 1][l] = piv[m + 1][l] - ratio * piv[m][l]
            for q in range(m + 2, 8):
                by0, by1 = piv[m][q] * inv0, piv[m + 1][q] * inv1
                for l in range(q, 8):
                    piv[q][l] = piv[q][l] - by0 * piv[m][l] - by1 * piv[m + 1][l]
                held[q] = held[q] - by0 * held[m] - by1 * held[m + 1]
                for t in tiles:
                    cols[t][q] = cols[t][q] - by0 * cols[t][m] - by1 * cols[t][m + 1]
        scaled = [held[m] * inv[m] for m in range(8)]
        for t in tiles:
            for m in range(8):
                col = cols[t][m]
                if t == home:
                    if m == 7:
                        continue
                    col = jnp.where(sub8 > m, col, 0.0)
                rows[t] = rows[t] - col * scaled[m]
    whole = jnp.concatenate(rows, axis=0)
    diag = jnp.sum(jnp.where(sub == lane, whole[:, :size], 0.0), axis=1, keepdims=True)
    return whole[:, size:] * (1.0 / jnp.sqrt(diag))


def inverse_factor(inner, work, out_ref, between):
    rank = inner.shape[0]
    sub = lax.broadcasted_iota(jnp.int32, (rank, rank), 0)
    lane = lax.broadcasted_iota(jnp.int32, (rank, rank), 1)
    same = sub == lane
    diag = jnp.where(same, inner, 0.0)
    tall = 1.0 / jnp.sqrt(jnp.sum(diag, axis=1, keepdims=True))
    wide = 1.0 / jnp.sqrt(jnp.sum(diag, axis=0, keepdims=True))
    work[:, :rank] = inner * tall * wide
    work[:, rank:] = jnp.where(same, 1.0, 0.0).astype(F32)
    for step, at in enumerate(range(0, rank, BLOCK)):
        inverse = eliminate(work[at : at + BLOCK, at : at + BLOCK])
        top = mul(inverse, work[at : at + BLOCK, :], NN)
        out_ref[at : at + BLOCK, :] = top[:, rank:] * wide
        if at + BLOCK < rank:
            left = top[:, at + BLOCK : rank]
            work[at + BLOCK :, :] = work[at + BLOCK :, :] - mul(left, top, TN)
        between(step, rank // BLOCK)


def kernel(
    n, h_ref, bx_ref, by_ref, out_ref,
    hw, ghi, glo, begin, bhi, blo, part, rslots, image, ipart, islots, inner, work, linv, fxt, fy, wsum, cpart, oslots, back_hi, back_lo, extra, final,
    own, bs, br, bzs, bzr, bps, bpr, xs, xr, zr, zl, ks, yr, rs, rr, as_, ar, ps, pr, i1s, i1r, i2s, i2r, fs, fr, os_, or_, fxs, fbs, gs, gr, es, er,
):
    i, j = lax.axis_index("gx"), lax.axis_index("gy")
    p, c = i // 2, lax.rem(i, 2)
    even = c == 0
    odd = c == 1
    slabs, hrows, hcols = h_ref.shape
    rank = bx_ref.shape[1]
    chunk = image.shape[3]
    side = rank // 2
    irows = 3 * side // n
    sibling = (i + 1 - 2 * c, j)

    def mod(v):
        return lax.rem(v + n, n)

    def rc(src, dst, ss, rsem, dev):
        return pltpu.make_async_remote_copy(
            src_ref=src, dst_ref=dst, send_sem=ss, recv_sem=rsem, device_id=dev, device_id_type=MESH
        )

    a = jnp.where(even, p, j)
    r = jnp.where(even, j, p)

    def dev(aa, rr_):
        return (jnp.where(even, 2 * aa, 2 * rr_ + 1), jnp.where(even, rr_, aa))

    def place(pp, jj):
        return jnp.where(even, pp, jj), jnp.where(even, jj, pp)

    corner = n == 4
    hops = (1, 2) if corner else tuple(range(1, n))
    far = (3,) if corner else hops

    def across(e):
        return (p + 1 - 2 * lax.rem(p, 2), lax.rem(p + 2, n), n - 1 - p)[e - 1]

    def peer(e):
        return across(e) if corner else mod(p + e)

    def source(e):
        return across(e) if corner else mod(p - e)

    barrier = pltpu.get_barrier_semaphore()
    for e in range(1, 2 * n):
        pl.semaphore_signal(barrier, inc=1, device_id=(lax.rem(i + e, 2 * n), j), device_id_type=MESH)
    for d in range(1, n):
        for cc in range(2):
            pl.semaphore_signal(barrier, inc=1, device_id=(2 * p + cc, mod(j + d)), device_id_type=MESH)
    pl.semaphore_wait(barrier, 2 * n - 1 + 2 * (n - 1))

    @pl.when(even)
    def _():
        for q in range(n // 2):
            begin[p, q] = bx_ref[q * chunk : (q + 1) * chunk, :]

    @pl.when(odd)
    def _():
        for q in range(n):
            begin[j, q] = by_ref[q * chunk : (q + 1) * chunk, :]
        for d in range(1, n):
            rc(begin.at[j, p], begin.at[j, p], bzs.at[d], bzr.at[d], (i, mod(j + d))).start()

    ykey = j * 2 + c

    width = hcols // 2
    pieces = [pl.ds(b * width, width) for b in range(2)]

    def right(src, s, b):
        to = (2 * p + 1, jnp.minimum(j + 1, n - 1))
        return rc(src.at[:, :, pieces[b]], hw.at[s, :, :, pieces[b]], zr.at[s, b], yr.at[s, b], to)

    def left(src, s, b):
        to = (2 * p + 1, jnp.maximum(j - 1, 0))
        return rc(src.at[:, :, pieces[b]], hw.at[s, :, :, pieces[b]], zl.at[s, b], yr.at[s, b], to)

    for b in range(2):
        pl.when(j < n - 1)(lambda: right(h_ref, ykey, b).start())
        pl.when(j > 0)(lambda: left(h_ref, ykey, b).start())

    def own_copy():
        return pltpu.make_async_copy(h_ref, hw.at[jnp.where(even, i, ykey)], own.at[0])

    own_copy().start()
    pl.when(even)(lambda: rc(h_ref, hw.at[ykey], ks.at[0], yr.at[ykey, 0], sibling).start())
    pl.when(odd)(lambda: rc(h_ref, hw.at[i], ks.at[0], xr.at[i, 0], sibling).start())

    half = n // 2

    bxc = bx_ref.reshape(half, chunk, rank)

    def start_x(e):
        dst = begin.at[p, pl.ds(c * half, half)]
        return rc(bxc, dst, bs.at[e], br.at[i, 0], (2 * (p if e == 0 else peer(e)), j))

    def plane_x(e):
        return rc(h_ref, hw.at[i], xs.at[e], xr.at[i, 0], (2 * peer(e), j))

    sh = slabs // 2

    def forward_x(e, q):
        slot = 2 * source(e) + q
        at = hw.at[slot, pl.ds((e - 1) * sh, sh)]
        return rc(at, at, fxs.at[e, q], xr.at[slot, e - 1], (2 * peer(3 - e), j))

    def forward_start(e, q):
        at = begin.at[source(e), q * half + e - 1]
        return rc(at, at, fbs.at[e, q], br.at[2 * source(e) + q, e - 1], (2 * peer(3 - e), j))

    pl.when(odd)(lambda: start_x(0).start())
    for e in hops:
        plane_x(e).start()
    for e in hops:
        start_x(e).start()
    own_copy().wait()

    @pl.when(even)
    def _():
        rc(h_ref, hw.at[i + 1], ks.at[0], xr.at[i + 1, 0], sibling).wait_recv()

        def cols(slot):
            for q in range(2):
                total = None
                for s in range(slabs):
                    term = bdot(hw[2 * p + q, s], hw[slot, s], NT)
                    total = term if total is None else total + term
                hi, lo = split(total)
                at = pl.ds(pl.multiple_of(slot * hrows, hrows), hrows)
                ghi[q * hrows : (q + 1) * hrows, at] = hi
                glo[q * hrows : (q + 1) * hrows, at] = lo

        def all_cols(slots):
            def step(t, carry):
                slot = slots[0]
                for u in range(1, len(slots)):
                    slot = jnp.where(t == u, slots[u], slot)
                cols(slot)
                return carry

            lax.fori_loop(0, len(slots), step, 0)

        for e in hops:
            for q in range(2):
                slot = 2 * source(e) + q
                rc(h_ref, hw.at[slot], ks.at[0], xr.at[slot, 0], sibling).wait_recv()
                if corner:
                    forward_x(e, q).start()
        all_cols([2 * p, 2 * p + 1] + [2 * source(e) + q for e in hops for q in range(2)])
        rc(bxc, begin.at[p, pl.ds(half, half)], ks.at[0], br.at[i + 1, 0], sibling).wait_recv()
        for e in hops:
            for q in range(2):
                pp = source(e)
                rc(bxc, begin.at[pp, pl.ds(q * half, half)], ks.at[0], br.at[2 * pp + q, 0], sibling).wait_recv()
                if corner:
                    forward_start(e, q).start()
        if corner:
            for q in range(2):
                slot = 2 * source(3) + q
                for b in range(2):
                    at = hw.at[slot, pl.ds(b * sh, sh)]
                    rc(at, at, ks.at[0], xr.at[slot, b], sibling).wait_recv()
            all_cols([2 * source(3), 2 * source(3) + 1])
            for q in range(2):
                for b in range(2):
                    at = begin.at[source(3), q * half + b]
                    rc(at, at, ks.at[0], br.at[2 * source(3) + q, b], sibling).wait_recv()

    def taken(s, first, last):
        return jnp.logical_or(jnp.logical_and(j == first, s > 1), jnp.logical_and(j == last, s < n - 2))

    def back_copies(to, s, b):
        at = pl.ds(pl.multiple_of(s * hcols + b * width, width), width)
        return [
            rc(src.at[s, :, pieces[b]], dst.at[:, at], gs.at[m, s, b], gr.at[m, s, b], (i, to))
            for m, (src, dst) in enumerate(((back_hi, ghi), (back_lo, glo)))
        ]

    @pl.when(odd)
    def _():
        for d in range(1, n):
            jj = mod(j - d)
            rc(begin.at[jj, p], begin.at[jj, p], bzs.at[0], bzr.at[d], sibling).wait_recv()
            for e in range(1, n):
                rc(begin.at[jj, p], begin.at[jj, p], bps.at[e, d], bpr.at[e, d], (2 * mod(p + e) + 1, j)).start()
        rc(h_ref, hw.at[j * 2], ks.at[0], yr.at[j * 2, 0], sibling).wait_recv()

        def cols(jj):
            total = None
            for q in range(2):
                for s in range(slabs):
                    term = bdot(hw[2 * j + q, s], hw[2 * jj + q, s], TN)
                    total = term if total is None else total + term
            hi, lo = split(total)
            at = pl.ds(pl.multiple_of(jj * hcols, hcols), hcols)
            ghi[:, at] = hi
            glo[:, at] = lo

        cols(j)

        def give_back(base, s, b):
            total = None
            for q in range(2):
                for t in range(slabs):
                    term = bdot(hw[2 * base + q, t], hw[2 * s + q, t, :, pieces[b]], TN)
                    total = term if total is None else total + term
            back_hi[s, :, pieces[b]], back_lo[s, :, pieces[b]] = split(total)
            for copy in back_copies(base, s, b):
                copy.start()

        def step(d, carry):
            low, high = jnp.maximum(j - d, 0), jnp.minimum(j + d, n - 1)
            from_low = jnp.logical_and(j - d >= 0, jnp.logical_or(d == 1, j < n - 1))
            from_high = jnp.logical_and(j + d < n, jnp.logical_or(d == 1, j > 0))
            for_first = jnp.logical_and(from_high, j == 1)
            for_last = jnp.logical_and(from_low, j == n - 2)
            for b in range(2):
                for q in range(2):
                    @pl.when(from_low)
                    def _():
                        s = low * 2 + q
                        right(hw.at[s], s, b).wait_recv()
                        pl.when(j < n - 2)(lambda: right(hw.at[s], s, b).start())

                    @pl.when(from_high)
                    def _():
                        s = high * 2 + q
                        left(hw.at[s], s, b).wait_recv()
                        pl.when(j > 1)(lambda: left(hw.at[s], s, b).start())

                pl.when(jnp.logical_and(for_first, d > 1))(lambda: give_back(0, high, b))
                pl.when(jnp.logical_and(for_last, d > 1))(lambda: give_back(n - 1, low, b))
            for b in range(2):
                pl.when(jnp.logical_and(for_first, d == 1))(lambda: give_back(0, high, b))
                pl.when(jnp.logical_and(for_last, d == 1))(lambda: give_back(n - 1, low, b))
            pl.when(from_low)(lambda: cols(low))
            pl.when(from_high)(lambda: cols(high))
            return carry

        lax.fori_loop(1, n, step, 0)
        for s in range(n):
            for b in range(2):
                @pl.when(taken(s, 0, n - 1))
                def _():
                    for copy in back_copies(j, s, b):
                        copy.wait_recv()

        for d in range(1, n):
            for e in range(1, n):
                at = begin.at[mod(j - d), mod(p - e)]
                rc(at, at, bzs.at[0], bpr.at[e, d], sibling).wait_recv()

    def reduce_copy(it, d):
        to = mod(r + d)
        return rc(part.at[it, to], rslots.at[it, d - 1], rs.at[it, d], rr.at[it, d], dev(a, to))

    def product(it):
        def block(to):
            at = pl.ds(pl.multiple_of(to * chunk, chunk), chunk)
            basis = bhi[...], blo[...]
            part[it, to] = dot3((ghi[at, :], glo[at, :]), basis, NN)

        for d in range(1, n):
            block(mod(r + d))
            reduce_copy(it, d).start()
        block(r)

    def spread_basis(source):
        def step(q, carry):
            at = pl.ds(pl.multiple_of(q * n * chunk, n * chunk), n * chunk)
            hi, lo = split(source(q).reshape(n * chunk, rank))
            bhi[at, :] = hi
            blo[at, :] = lo
            return carry

        lax.fori_loop(0, n, step, 0)

    def turned(it, turn):
        return lambda q: dot3(split(image[it, q].reshape(n * chunk, rank)), turn, NT)

    spread_basis(lambda q: begin[q])
    product(0)

    def line_copy(it, d, src_j, to_j):
        q, w = place(p, src_j)
        return rc(image.at[it, q, w], image.at[it, q, w], as_.at[it, d], ar.at[it, d], (i, to_j))

    def plane_copy(it, e, d):
        q, w = place(p, mod(j - d))
        return rc(image.at[it, q, w], image.at[it, q, w], ps.at[it, e, d], pr.at[it, e, d], (2 * peer(e) + c, j))

    def half_copy(it, e, d):
        q, w = place(source(e), mod(j - d))
        at = image.at[it, q, w, pl.ds((e - 1) * (chunk // 2), chunk // 2)]
        return rc(at, at, ps.at[it, 0 if e == 1 else 3, d], pr.at[it, 0 if e == 1 else 3, d], (2 * peer(3 - e) + c, j))

    def forward(it, d):
        if corner:
            for e in hops:
                q, w = place(source(e), mod(j - d))
                at = image.at[it, q, w]
                rc(at, at, ps.at[it, e, d], pr.at[it, e, d], sibling).wait_recv()
                half_copy(it, e, d).start()

    def arriving(it, e, d):
        q, w = place(source(e), mod(j - d))
        if not corner:
            return [(image.at[it, q, w], ps.at[it, e, d], pr.at[it, e, d])]
        return [
            (image.at[it, q, w, pl.ds(b * (chunk // 2), chunk // 2)], ps.at[it, 3 * b, d], pr.at[it, 3 * b, d])
            for b in range(2)
        ]

    def inner_one(it, e):
        to = mod(p + e)
        return rc(ipart.at[it, to], islots.at[it, e - 1], i1s.at[it, e], i1r.at[it, e], (2 * to + c, j))

    def inner_two(it, e):
        return rc(inner.at[it, p], inner.at[it, p], i2s.at[it, e], i2r.at[it, e], (2 * mod(p + e) + c, j))

    def iteration(it, carry):
        for d in range(1, n):
            reduce_copy(it, d).wait_recv()
        total = part[it, r]
        for d in range(1, n):
            total = total + rslots[it, d - 1]
        image[it, a, r] = total
        for d in range(1, n):
            line_copy(it, d, j, mod(j + d)).start()
        spread_needed = jnp.logical_or(odd, it < ITERS - 1)

        @pl.when(spread_needed)
        def _():
            for e in hops:
                plane_copy(it, e, 0).start()

        top, low = mul(total[:, :side], total, TN), mul(total[:, side:], total[:, side:], TN)
        for d in range(1, n):
            line_copy(it, d, mod(j - d), j).wait_recv()
            q, w = place(p, mod(j - d))
            if d == 1:
                @pl.when(spread_needed)
                def _():
                    for e in hops:
                        plane_copy(it, e, 1).start()

            rows = image[it, q, w]
            top = top + mul(rows[:, :side], rows, TN)
            low = low + mul(rows[:, side:], rows[:, side:], TN)
        ipart[it] = jnp.concatenate([top[:, :side], top[:, side:], low], axis=0).reshape(n, irows, side)
        for e in range(1, n):
            inner_one(it, e).start()
        pl.when(spread_needed)(lambda: forward(it, 0))
        for e in range(1, n):
            inner_one(it, e).wait_recv()
        total = ipart[it, p]
        for e in range(1, n):
            total = total + islots[it, e - 1]
        inner[it, p] = total
        for e in range(1, n):
            inner_two(it, e).start()

        @pl.when(spread_needed)
        def _():
            for d in range(2, n):
                for e in hops:
                    plane_copy(it, e, d).start()

        for e in range(1, n):
            at = inner.at[it, mod(p - e)]
            rc(at, at, i2s.at[it, e], i2r.at[it, e], sibling).wait_recv()

        def between(step, steps):
            for d in range(1, n):
                if min(d - 1, steps - 1) == step:
                    pl.when(spread_needed)(lambda: forward(it, d))

        flat = inner[it].reshape(3 * side, side)
        upper = flat[side : 2 * side]
        whole = jnp.concatenate([
            jnp.concatenate([flat[:side], upper], axis=1), jnp.concatenate([upper.T, flat[2 * side :]], axis=1),
        ], axis=0)
        inverse_factor(whole, work, linv, between)

        @pl.when(spread_needed)
        def _():
            for d in range(n):
                for e in far:
                    for at in arriving(it, e, d):
                        rc(at[0], at[0], at[1], at[2], sibling).wait_recv()


        @pl.when(it < ITERS - 1)
        def _():
            turn = split(linv[...])
            spread_basis(turned(it, turn))
            product(jnp.minimum(it + 1, ITERS - 1))

        for d in range(1, n):
            reduce_copy(it, d).wait_send()
            line_copy(it, d, j, mod(j + d)).wait_send()
        for e in range(1, n):
            inner_one(it, e).wait_send()
            inner_two(it, e).wait_send()

        @pl.when(spread_needed)
        def _():
            for d in range(n):
                for e in hops:
                    plane_copy(it, e, d).wait_send()
                    if corner:
                        half_copy(it, e, d).wait_send()

        return carry

    lax.fori_loop(0, ITERS, iteration, 0)

    last = ITERS - 1
    arows, bcols = out_ref.shape[1], out_ref.shape[2]
    give = rc(fxt, fxt, fs.at[0], fr.at[0], sibling)

    @pl.when(even)
    def _():
        turn = split(linv[...])
        rows = image[last, p].reshape(n * chunk, rank)
        fxt[...] = dot3(turn, split(rows), NT).astype(BF16)
        give.start()

    def part_copy(to):
        return rc(cpart.at[to], oslots.at[p], os_.at[to], or_.at[p], (to, j))

    middle = jnp.logical_and(j > 0, j < n - 1)
    work_here = jnp.logical_and(odd, middle)
    beside = jnp.logical_or(j == 1, j == n - 2)
    end = jnp.where(j <= 1, 0, n - 1)

    @pl.when(work_here)
    def _():
        mine = linv[pl.ds(pl.multiple_of(j * bcols, bcols), bcols), :]
        other = linv[pl.ds(pl.multiple_of(end * bcols, bcols), bcols), :]
        turn = split(jnp.concatenate([mine, other], axis=0))

        def step(q, carry):
            at = pl.ds(pl.multiple_of(q * n * chunk, n * chunk), n * chunk)
            fy[at, :] = turned(last, turn)(q).astype(BF16)
            return carry

        lax.fori_loop(0, n, step, 0)
        for q in range(2):
            for s in range(slabs):
                total = None
                for jj in range(n):
                    term = bdot(hw[2 * jj + q, s], fy[jj * hcols : (jj + 1) * hcols, :], NN)
                    total = term if total is None else total + term
                wsum[q, s] = total
        give.wait_recv()
        for s in range(slabs):
            total = None
            for q in range(2):
                tall = fxt[:, q * hrows : (q + 1) * hrows]
                hi, lo = split(wsum[q, s])
                term = bdot(tall, hi, NN) + bdot(tall, lo, NN)
                total = term if total is None else total + term
            for to in range(2 * n):
                cpart[to, s] = total[to * arows : (to + 1) * arows, :]
        for e in range(1, 2 * n):
            part_copy(lax.rem(i + e, 2 * n)).start()
        oslots[p] = cpart[i]

    pl.when(jnp.logical_and(odd, jnp.logical_not(middle)))(lambda: give.wait_recv())
    hand = rc(extra, final, es.at[0], er.at[0], (i, end))

    @pl.when(middle)
    def _():
        for pp in range(n):
            @pl.when(jnp.logical_or(even, p != pp))
            def _():
                rc(oslots.at[pp], oslots.at[pp], fs.at[0], or_.at[pp], sibling).wait_recv()

        total = oslots[0]
        for pp in range(1, n):
            total = total + oslots[pp]
        out_ref[...] = total[:, :, :bcols]
        extra[...] = total[:, :, bcols:]
        pl.when(beside)(lambda: hand.start())

    @pl.when(jnp.logical_not(middle))
    def _():
        hand.wait_recv()
        out_ref[...] = final[...]

    pl.when(even)(lambda: give.wait_send())
    pl.when(jnp.logical_and(middle, beside))(lambda: hand.wait_send())
    pl.when(even)(lambda: rc(h_ref, hw.at[ykey], ks.at[0], yr.at[ykey, 0], sibling).wait_send())
    pl.when(odd)(lambda: rc(h_ref, hw.at[i], ks.at[0], xr.at[i, 0], sibling).wait_send())
    pl.when(odd)(lambda: start_x(0).wait_send())
    for e in hops:
        plane_x(e).wait_send()
        start_x(e).wait_send()
    for b in range(2):
        pl.when(j < n - 1)(lambda: right(h_ref, ykey, b).wait_send())
        pl.when(j > 0)(lambda: left(h_ref, ykey, b).wait_send())

    if corner:
        @pl.when(even)
        def _():
            for e in hops:
                for q in range(2):
                    forward_x(e, q).wait_send()
                    forward_start(e, q).wait_send()

    @pl.when(work_here)
    def _():
        for e in range(1, 2 * n):
            part_copy(lax.rem(i + e, 2 * n)).wait_send()

    @pl.when(odd)
    def _():
        for d in range(1, n):
            rc(begin.at[j, p], begin.at[j, p], bzs.at[d], bzr.at[d], (i, mod(j + d))).wait_send()
            for e in range(1, n):
                at = begin.at[mod(j - d), p]
                rc(at, at, bps.at[e, d], bpr.at[e, d], (2 * mod(p + e) + 1, j)).wait_send()
        for s in range(n):
            for b in range(2):
                @pl.when(taken(s, 1, n - 2))
                def _():
                    for copy in back_copies(jnp.where(j == 1, 0, n - 1), s, b):
                        copy.wait_send()

        for d in range(1, n):
            for b in range(2):
                for q in range(2):
                    @pl.when(jnp.logical_and(j - d >= 0, j < n - 2))
                    def _():
                        s = jnp.maximum(j - d, 0) * 2 + q
                        right(hw.at[s], s, b).wait_send()

                    @pl.when(jnp.logical_and(j + d < n, j > 1))
                    def _():
                        s = jnp.minimum(j + d, n - 1) * 2 + q
                        left(hw.at[s], s, b).wait_send()


def on_device(history, start_x, start_y):
    nx, n = lax.axis_size("gx"), lax.axis_size("gy")
    slabs, hrows, hcols = history.shape
    rank = start_x.shape[1]
    rows = 2 * hrows
    assert nx == 2 * n and rows == hcols and n % 2 == 0 and n > 3 and slabs % 2 == 0
    chunk = rows // n
    dma = pltpu.SemaphoreType.DMA
    vmem = pltpu.VMEM
    arows, bcols = rank // nx, rank // n
    piece = (3 * (rank // 2) // n, rank // 2)
    shape, pair = (slabs, arows, bcols), (slabs, arows, 2 * bcols)
    scratch = [
        vmem((2 * n, slabs, hrows, hcols), BF16),
        vmem((rows, n * rows), BF16), vmem((rows, n * rows), BF16),
        vmem((n, n, chunk, rank), F32),
        vmem((n * rows, rank), BF16), vmem((n * rows, rank), BF16),
        vmem((ITERS, n, chunk, rank), F32),
        vmem((ITERS, n - 1, chunk, rank), F32),
        vmem((ITERS, n, n, chunk, rank), F32),
        vmem((ITERS, n) + piece, F32),
        vmem((ITERS, n - 1) + piece, F32),
        vmem((ITERS, n) + piece, F32),
        vmem((rank, 2 * rank), F32),
        vmem((rank, rank), F32),
        vmem((rank, rows), BF16),
        vmem((n * rows, 2 * bcols), BF16),
        vmem((2, slabs, hrows, 2 * bcols), F32),
        vmem((nx,) + pair, F32),
        vmem((n,) + pair, F32),
        vmem((n, rows, hcols), BF16), vmem((n, rows, hcols), BF16),
        vmem(shape, F32), vmem(shape, F32),
        dma((1,)),
        dma((n,)), dma((nx, 2)),
        dma((n,)), dma((n,)),
        dma((n, n)), dma((n, n)),
        dma((n,)), dma((nx, 2)),
        dma((nx, 2)), dma((nx, 2)), dma((1,)), dma((nx, 2)),
        dma((ITERS, n)), dma((ITERS, n)),
        dma((ITERS, n)), dma((ITERS, n)),
        dma((ITERS, n, n)), dma((ITERS, n, n)),
        dma((ITERS, n)), dma((ITERS, n)),
        dma((ITERS, n)), dma((ITERS, n)),
        dma((1,)), dma((1,)),
        dma((nx,)), dma((n,)),
        dma((3, 2)), dma((3, 2)),
        dma((2, n, 2)), dma((2, n, 2)),
        dma((1,)), dma((1,)),
    ]
    return pl.pallas_call(
        functools.partial(kernel, n),
        out_shape=jax.ShapeDtypeStruct(shape, F32),
        in_specs=[pl.BlockSpec(memory_space=pl.ANY)] + [pl.BlockSpec(memory_space=pltpu.VMEM)] * 2,
        out_specs=pl.BlockSpec(memory_space=pltpu.VMEM),
        scratch_shapes=scratch,
        compiler_params=pltpu.CompilerParams(
            collective_id=0, has_side_effects=True, vmem_limit_bytes=56 * 1024 * 1024
        ),
        name="tucker",
    )(history, start_x, start_y)


def solution(mesh):
    return jax.shard_map(
        on_device,
        mesh=mesh,
        in_specs=(P(None, "gx", "gy"), P("gx", None), P("gy", None)),
        out_specs=P(None, "gx", "gy"),
        check_vma=False,
    )
```
